256 devices in a mesh: cuts: 2 (over core), tile: 128 (over z, y, x).
Axes of the slice: x: 4, y: 4, z: 8, core: 2. Of those that a mesh axis runs over, the one named last changes fastest.
Arguments:
- object_slices: float32 [2, 2, 16384, 2048], P('cuts', None, 'tile'), may hold values from -1 to 1, as said below
- probe: float32 [2, 256, 256], replicated, may hold values from -4 to 4
- positions: int32 [256, 2], P('tile'), may hold values from 0 to 16128, as said below
- counts: int32 [128], P('tile'), may hold values from 1 to 2
- intensity: float32 [256, 256, 256], P('tile'), may hold values from 0 to 2
Outputs:
- object_grad: float32 [2, 2, 16384, 2048], P('cuts', None, 'tile')
The draws below stay inside these ranges and needn't reach their ends.
Inputs may be any that keep to these rules, and one draw needn't show every extreme that they name: `positions`: slot s belongs to strip t = s // 2; its row offset lies between max(0, (t - 1) * 128) and min(t * 128, 16128), its column offset between 0 and 1792. `object_slices`: every object cell has a magnitude between 0.7 and 1.0.
All inputs are finite; a program needn't handle non-finite values.
Results may differ from the reference program's by a relative error of at most 0.00015.
Values sent between devices are 32-bit elements; how exact they have to be, the bound alone decides.
No kernel may reach another device: no remote copies, remote signals or barrier semaphores. Data moves between devices by JAX's collectives and lax.ppermute only.
A program may use at most 64 MiB of HBM per device.

```python
import math
import jax
import jax.numpy as jnp
from jax import lax

WIN = 256
STRIP = 128
NCOL = 2048
POS_CAP = 2
TILES = 128
SLICES = 2
NROW = 16384
SLOTS = 256


def draw_object_slices(key, part):
    amp_key, phase_key = jax.random.split(jax.random.fold_in(key, 11))
    shape = (SLICES, NROW, NCOL)
    amplitude = jax.random.uniform(amp_key, shape, jnp.float32, 0.75, 1.0)
    phase = jax.random.uniform(phase_key, shape, jnp.float32, -math.pi, math.pi)
    return jnp.stack([amplitude * jnp.cos(phase), amplitude * jnp.sin(phase)], axis=1)


def draw_positions(key, part):
    row_key, col_key, pick_key = jax.random.split(jax.random.fold_in(key, 23), 3)
    owner = jnp.arange(SLOTS, dtype=jnp.int32) // POS_CAP
    lowest = jnp.maximum(0, (owner - 1) * STRIP)
    highest = jnp.minimum(owner * STRIP, NROW - WIN)
    raw_rows = jax.random.randint(row_key, (SLOTS,), 0, STRIP + 1, dtype=jnp.int32)
    row_starts = lowest + raw_rows % (highest - lowest + 1)
    col_starts = jax.random.randint(col_key, (SLOTS,), 0, NCOL - WIN + 1, dtype=jnp.int32)
    chosen = jax.random.permutation(pick_key, SLOTS)
    col_starts = col_starts.at[chosen[0]].set(0).at[chosen[1]].set(NCOL - WIN)
    return jnp.stack([row_starts, col_starts], axis=1)


def draw_counts(key, part):
    base_key, pick_key = jax.random.split(jax.random.fold_in(key, 37))
    drawn = jax.random.randint(base_key, (TILES,), 1, POS_CAP // 2 + 1, dtype=jnp.int32)
    busiest = jax.random.randint(pick_key, (), 0, TILES, dtype=jnp.int32)
    return drawn.at[busiest].set(POS_CAP)


def shard_levels(key, extent, cuts, smallest, top_value):
    gain = 1.0
    for dim, parts in cuts:
        draws = jax.random.uniform(jax.random.fold_in(jax.random.fold_in(key, 6), dim), (parts,), jnp.float32, smallest / len(cuts), top_value / len(cuts))
        gain = gain * jnp.repeat(jnp.exp(draws), extent[dim] // parts).reshape((-1,) + (1,) * (len(extent) - 1 - dim))
    return gain


def scatter_about(own_key, extent, scale, bound, kind=jnp.bfloat16):
    values = scale * jax.random.normal(own_key, extent, jnp.float32)
    return jnp.clip(values, min=-bound, max=bound).astype(kind)


def setup_inputs(seed: int = 0) -> dict:
    streams_of = jax.random.split(jax.random.key(seed), 6)
    object_slices = draw_object_slices(jax.random.fold_in(streams_of[5], 71), 0)
    probe = scatter_about(streams_of[1], (2, WIN, WIN), 0.7, 4.0, jnp.float32)
    positions = draw_positions(jax.random.fold_in(streams_of[5], 71), 0)
    counts = draw_counts(jax.random.fold_in(streams_of[5], 71), 0)
    intensity = jnp.clip(2.0 * jax.random.uniform(streams_of[4], (SLOTS, WIN, WIN), jnp.float32) ** shard_levels(streams_of[4], (SLOTS, WIN, WIN), ((0, 128),), -0.2, 0.2), 0.0, 2.0)
    return dict(object_slices=object_slices, probe=probe, positions=positions, counts=counts, intensity=intensity)


def kernel_phase(window):
    frequency = jnp.arange(window, dtype=jnp.int32)
    centred = (frequency + window // 2) % window - window // 2
    wrapped = (centred * centred) % (4 * window)
    return wrapped.astype(jnp.float32) * (math.pi / (2 * window))


def reference(object_slices, probe, positions, counts, intensity):
    angle = kernel_phase(WIN)
    filter_one = lax.complex(jnp.cos(angle), -jnp.sin(angle))
    filter_two = filter_one[:, None] * filter_one[None, :]
    probe_field = lax.complex(probe[0], probe[1])
    object_field = lax.complex(object_slices[:, 0], object_slices[:, 1])

    def forward_prop(field_in):
        return jnp.fft.ifft2(jnp.fft.fft2(field_in) * filter_two)

    def adjoint_prop(field_in):
        return jnp.fft.ifft2(jnp.fft.fft2(field_in) * jnp.conj(filter_two))

    def one_slot(slot_index, gradient):
        row_start = positions[slot_index, 0].astype(jnp.int32)
        col_start = positions[slot_index, 1].astype(jnp.int32)
        live_weight = (slot_index % POS_CAP < counts[slot_index // POS_CAP]).astype(jnp.float32)
        start = (jnp.int32(0), row_start, col_start)
        patches = lax.dynamic_slice(object_field, start, (SLICES, WIN, WIN))
        wave_now = probe_field
        entering = []
        for layer in range(SLICES):
            entering.append(wave_now)
            wave_now = wave_now * patches[layer]
            if layer + 1 < SLICES:
                wave_now = forward_prop(wave_now)
        far_field = jnp.fft.fft2(wave_now, norm="ortho")
        modelled = jnp.real(far_field) ** 2 + jnp.imag(far_field) ** 2
        residual = (modelled - intensity[slot_index]) * live_weight
        back_wave = jnp.fft.ifft2(far_field * residual, norm="ortho")
        terms = []
        for layer in reversed(range(SLICES)):
            terms.append(jnp.conj(entering[layer]) * back_wave)
            back_wave = jnp.conj(patches[layer]) * back_wave
            if layer > 0:
                back_wave = adjoint_prop(back_wave)
        stacked = jnp.stack(terms[::-1])
        current = lax.dynamic_slice(gradient, start, (SLICES, WIN, WIN))
        return lax.dynamic_update_slice(gradient, current + stacked, start)

    gradient = lax.fori_loop(0, positions.shape[0], one_slot, jnp.zeros_like(object_field))
    return jnp.stack([jnp.real(gradient), jnp.imag(gradient)], axis=1)
```

```python
import numpy as np
import ml_dtypes

import jax
import jax.numpy as jnp
from jax import lax
from jax.experimental import pallas as pl
from jax.experimental.pallas import tpu as pltpu
from jax.sharding import PartitionSpec as P

WIN = 256
HALF = 128


def split_tables(real_part, imag_part):
    parts = []
    for values in (real_part, imag_part - real_part, real_part + imag_part):
        high = values.astype(ml_dtypes.bfloat16)
        low = (values - high.astype(np.float64)).astype(ml_dtypes.bfloat16)
        parts += [high, low]
    return np.stack(parts)


def build_tables():
    index = np.arange(WIN)
    turned = 2.0 * np.pi * ((index[:, None] * index[None, :]) % WIN) / WIN
    dft = (np.cos(turned) - 1j * np.sin(turned)) / np.sqrt(WIN)
    centred = (index + WIN // 2) % WIN - WIN // 2
    phase = np.pi * (centred * centred % (4 * WIN)) / (2 * WIN)
    prop = np.conj(dft) @ ((np.cos(phase) - 1j * np.sin(phase))[:, None] * dft)
    prop = 0.5 * (prop + prop.T)
    return split_tables(dft.real, dft.imag), split_tables(prop.real, prop.imag)


def split(value):
    high = value.astype(jnp.bfloat16)
    low = (value - high.astype(jnp.float32)).astype(jnp.bfloat16)
    return high, low


def dot(left, right):
    return jnp.dot(left, right, preferred_element_type=jnp.float32)


def product(field, table, which, from_left):
    high, low = split(field)
    table_high = table[2 * which]
    table_low = table[2 * which + 1]
    if from_left:
        return dot(table_high, high) + (dot(table_high, low) + dot(table_low, high))
    return dot(high, table_high) + (dot(low, table_high) + dot(high, table_low))


def complex_product(real, imag, table, conjugate, from_left):
    shared = product(real + imag, table, 0, from_left)
    if conjugate:
        first = product(real, table, 2, from_left)
        second = product(imag, table, 1, from_left)
        return shared + second, shared - first
    first = product(real, table, 1, from_left)
    second = product(imag, table, 2, from_left)
    return shared - second, shared + first


def sandwich(real, imag, table, conjugate):
    real, imag = complex_product(real, imag, table, conjugate, False)
    return complex_product(real, imag, table, conjugate, True)


def block(number):
    return pl.ds(pl.multiple_of(number * HALF, HALF), HALF)


def cut_piece(strip_ref, column, out_ref):
    first = lax.shift_right_logical(column, 7)
    offset = jnp.bitwise_and(column, HALF - 1)
    lanes = lax.broadcasted_iota(jnp.int32, (HALF, HALF), 1)
    mine = lanes >= offset
    third = jnp.minimum(first + 2, strip_ref.shape[-1] // HALF - 1)
    for part in range(2):
        out_ref[part, :, 0:HALF] = jnp.where(
            mine, strip_ref[0, part, :, block(first)], strip_ref[0, part, :, block(third)]
        )
        out_ref[part, :, HALF:WIN] = strip_ref[0, part, :, block(first + 1)]


def own_kernel(pos_ref, strip_ref, same_ref, cross_ref):
    core = lax.axis_index("cuts")
    cut_piece(strip_ref, pos_ref[core, 1], same_ref)
    cut_piece(strip_ref, pos_ref[1 - core, 1], cross_ref)


def halo_kernel(
    below_ref, above_ref, strip_ref, up_same_ref, up_cross_ref, down_same_ref, down_cross_ref
):
    core = lax.axis_index("cuts")
    cut_piece(strip_ref, above_ref[core, 1], up_same_ref)
    cut_piece(strip_ref, above_ref[1 - core, 1], up_cross_ref)
    cut_piece(strip_ref, below_ref[core, 1], down_same_ref)
    cut_piece(strip_ref, below_ref[1 - core, 1], down_cross_ref)


def slot_kernel(
    pos_ref,
    counts_ref,
    probe_ref,
    dft_ref,
    prop_ref,
    own_same_ref,
    own_cross_ref,
    low_same_ref,
    low_cross_ref,
    high_same_ref,
    high_cross_ref,
    intensity_ref,
    rim_same_ref,
    rim_cross_ref,
    mid_same_ref,
    mid_cross_ref,
    object_ref,
    grad_ref,
    measured_ref,
    sem,
):
    core = lax.axis_index("cuts")
    tile = lax.axis_index("tile")
    live = counts_ref[0] > core

    @pl.when(live)
    def _():
        fetch = pltpu.make_async_copy(intensity_ref.at[core], measured_ref, sem)
        fetch.start()
        shift_rows = pos_ref[core, 0] - (tile - 1) * HALF
        shift_cols = jnp.bitwise_and(pos_ref[core, 1], HALF - 1)
        rows = lax.broadcasted_iota(jnp.int32, (HALF, WIN), 0)
        from_low = rows >= shift_rows
        for part in range(2):
            object_ref[core, part, 0:HALF] = jnp.where(
                from_low, low_same_ref[part], high_same_ref[part]
            )
            object_ref[core, part, HALF:WIN] = own_same_ref[part]
            object_ref[1 - core, part, 0:HALF] = jnp.where(
                from_low, low_cross_ref[part], high_cross_ref[part]
            )
            object_ref[1 - core, part, HALF:WIN] = own_cross_ref[part]

        def rolled(part):
            return pltpu.roll(pltpu.roll(probe_ref[part], shift_rows, 0), shift_cols, 1)

        zero_re, zero_im = rolled(0), rolled(1)
        cell_re, cell_im = object_ref[0, 0], object_ref[0, 1]
        one_re, one_im = sandwich(
            zero_re * cell_re - zero_im * cell_im,
            zero_re * cell_im + zero_im * cell_re,
            prop_ref,
            False,
        )
        cell_re, cell_im = object_ref[1, 0], object_ref[1, 1]
        far_re, far_im = sandwich(
            one_re * cell_re - one_im * cell_im,
            one_re * cell_im + one_im * cell_re,
            dft_ref,
            False,
        )
        fetch.wait()
        residual = far_re * far_re + far_im * far_im - measured_ref[...]
        back_re, back_im = sandwich(far_re * residual, far_im * residual, dft_ref, True)
        grad_ref[1, 0] = one_re * back_re + one_im * back_im
        grad_ref[1, 1] = one_re * back_im - one_im * back_re
        back_re, back_im = sandwich(
            cell_re * back_re + cell_im * back_im,
            cell_re * back_im - cell_im * back_re,
            prop_ref,
            True,
        )
        grad_ref[0, 0] = zero_re * back_re + zero_im * back_im
        grad_ref[0, 1] = zero_re * back_im - zero_im * back_re

    @pl.when(jnp.logical_not(live))
    def _():
        grad_ref[...] = jnp.zeros_like(grad_ref)

    rim_same_ref[...] = grad_ref[core, :, 0:HALF]
    mid_same_ref[...] = grad_ref[core, :, HALF:WIN]
    rim_cross_ref[...] = grad_ref[1 - core, :, 0:HALF]
    mid_cross_ref[...] = grad_ref[1 - core, :, HALF:WIN]


def add_piece(out_ref, piece_ref, column, keep):
    first = lax.shift_right_logical(column, 7)
    offset = jnp.bitwise_and(column, HALF - 1)
    lanes = lax.broadcasted_iota(jnp.int32, (HALF, HALF), 1)
    mine = lanes >= offset
    third = jnp.minimum(first + 2, out_ref.shape[-1] // HALF - 1)
    for part in range(2):
        left = piece_ref[part, :, 0:HALF]
        right = piece_ref[part, :, HALF:WIN]
        if keep is not None:
            left = jnp.where(keep, left, 0.0)
            right = jnp.where(keep, right, 0.0)
        out_ref[0, part, :, block(first)] += jnp.where(mine, left, 0.0)
        out_ref[0, part, :, block(first + 1)] += right
        out_ref[0, part, :, block(third)] += jnp.where(mine, 0.0, left)


def collect_kernel(
    pos_ref,
    below_ref,
    above_ref,
    mid_same_ref,
    mid_cross_ref,
    up_same_ref,
    up_cross_ref,
    down_same_ref,
    down_cross_ref,
    out_ref,
):
    core = lax.axis_index("cuts")
    tile = lax.axis_index("tile")
    last = lax.axis_size("tile") - 1
    out_ref[...] = jnp.zeros_like(out_ref)
    add_piece(out_ref, mid_same_ref, pos_ref[core, 1], None)
    add_piece(out_ref, mid_cross_ref, pos_ref[1 - core, 1], None)
    rows = lax.broadcasted_iota(jnp.int32, (HALF, HALF), 0)
    below = jnp.where(tile == 0, last, tile - 1)
    above = jnp.where(tile == last, 0, tile + 1)
    for slot, piece_ref in ((core, up_same_ref), (1 - core, up_cross_ref)):
        shift_rows = below_ref[slot, 0] - (below - 1) * HALF
        add_piece(out_ref, piece_ref, below_ref[slot, 1], rows < shift_rows)
    for slot, piece_ref in ((core, down_same_ref), (1 - core, down_cross_ref)):
        shift_rows = above_ref[slot, 0] - (above - 1) * HALF
        add_piece(out_ref, piece_ref, above_ref[slot, 1], rows >= shift_rows)


SMEM = pl.BlockSpec(memory_space=pltpu.SMEM)
VMEM = pl.BlockSpec(memory_space=pltpu.VMEM)
ANY = pl.BlockSpec(memory_space=pl.ANY)


def cost(flops, moved):
    return pl.CostEstimate(flops=flops, bytes_accessed=moved, transcendentals=0)


def local(object_slices, probe, positions, counts, intensity):
    tiles = lax.axis_size("tile")

    def hop(value, swap, by):
        pairs = []
        for core in range(2):
            for tile in range(tiles):
                target = (core + swap) % 2 * tiles + (tile + by) % tiles
                pairs.append((core * tiles + tile, target))
        return lax.ppermute(value, ("cuts", "tile"), pairs)

    piece = jax.ShapeDtypeStruct((2, HALF, WIN), jnp.float32)
    dft, prop = build_tables()
    below = hop(positions, 0, 1)
    above = hop(positions, 0, -1)
    own_same, to_sibling = pl.pallas_call(
        own_kernel,
        out_shape=(piece,) * 2,
        in_specs=[SMEM, VMEM],
        out_specs=(VMEM,) * 2,
        cost_estimate=cost(0, 3 << 20),
        name="cut_own",
    )(positions, object_slices)
    up_same, up_cross, down_same, down_cross = pl.pallas_call(
        halo_kernel,
        out_shape=(piece,) * 4,
        in_specs=[SMEM, SMEM, VMEM],
        out_specs=(VMEM,) * 4,
        cost_estimate=cost(0, 3 << 20),
        name="cut_halo",
    )(below, above, object_slices)
    low_same = hop(up_same, 0, 1)
    high_same = hop(down_same, 0, -1)
    low_cross = hop(up_cross, 1, 1)
    high_cross = hop(down_cross, 1, -1)
    own_cross = hop(to_sibling, 1, 0)
    rim_same, rim_cross, mid_same, mid_cross = pl.pallas_call(
        slot_kernel,
        out_shape=(piece,) * 4,
        in_specs=[SMEM, SMEM] + [VMEM] * 9 + [ANY],
        out_specs=(VMEM,) * 4,
        scratch_shapes=[
            pltpu.VMEM((2, 2, WIN, WIN), jnp.float32),
            pltpu.VMEM((2, 2, WIN, WIN), jnp.float32),
            pltpu.VMEM((WIN, WIN), jnp.float32),
            pltpu.SemaphoreType.DMA,
        ],
        compiler_params=pltpu.CompilerParams(vmem_limit_bytes=32 << 20),
        cost_estimate=cost(72 * 2 * WIN**3, 6 << 20),
        name="slot",
    )(
        positions,
        counts,
        probe,
        jnp.asarray(dft),
        jnp.asarray(prop),
        own_same,
        own_cross,
        low_same,
        low_cross,
        high_same,
        high_cross,
        intensity,
    )
    got_up_same = hop(rim_same, 0, 1)
    got_down_same = hop(rim_same, 0, -1)
    got_up_cross = hop(rim_cross, 1, 1)
    got_down_cross = hop(rim_cross, 1, -1)
    got_mid = hop(mid_cross, 1, 0)
    return pl.pallas_call(
        collect_kernel,
        out_shape=jax.ShapeDtypeStruct(object_slices.shape, jnp.float32),
        in_specs=[SMEM] * 3 + [VMEM] * 6,
        out_specs=VMEM,
        compiler_params=pltpu.CompilerParams(vmem_limit_bytes=32 << 20),
        cost_estimate=cost(0, 4 << 20),
        name="collect",
    )(
        positions,
        below,
        above,
        mid_same,
        got_mid,
        got_up_same,
        got_up_cross,
        got_down_same,
        got_down_cross,
    )


def solution(mesh):
    in_specs = (
        P("cuts", None, "tile", None),
        P(),
        P("tile", None),
        P("tile"),
        P("tile", None, None),
    )
    out_specs = P("cuts", None, "tile", None)
    return jax.shard_map(local, mesh=mesh, in_specs=in_specs, out_specs=out_specs, check_vma=False)
```

```python
import numpy as np
import ml_dtypes

import jax
import jax.numpy as jnp
from jax import lax
from jax.experimental import pallas as pl
from jax.experimental.pallas import tpu as pltpu
from jax.sharding import PartitionSpec as P

WIN = 256
HALF = 128


def split_tables(real_part, imag_part):
    parts = []
    for values in (real_part, imag_part - real_part, real_part + imag_part):
        high = values.astype(ml_dtypes.bfloat16)
        low = (values - high.astype(np.float64)).astype(ml_dtypes.bfloat16)
        parts += [high, low]
    return np.stack(parts)


def build_tables():
    index = np.arange(WIN)
    turned = 2.0 * np.pi * ((index[:, None] * index[None, :]) % WIN) / WIN
    dft = (np.cos(turned) - 1j * np.sin(turned)) / np.sqrt(WIN)
    centred = (index + WIN // 2) % WIN - WIN // 2
    phase = np.pi * (centred * centred % (4 * WIN)) / (2 * WIN)
    prop = np.conj(dft) @ ((np.cos(phase) - 1j * np.sin(phase))[:, None] * dft)
    prop = 0.5 * (prop + prop.T)
    return split_tables(dft.real, dft.imag), split_tables(prop.real, prop.imag)


def split(value):
    high = value.astype(jnp.bfloat16)
    low = (value - high.astype(jnp.float32)).astype(jnp.bfloat16)
    return high, low


def dot(left, right):
    return jnp.dot(left, right, preferred_element_type=jnp.float32)


def product(field, table, which, from_left):
    high, low = split(field)
    table_high = table[2 * which]
    table_low = table[2 * which + 1]
    if from_left:
        return dot(table_high, high) + (dot(table_high, low) + dot(table_low, high))
    return dot(high, table_high) + (dot(low, table_high) + dot(high, table_low))


def complex_product(real, imag, table, conjugate, from_left):
    shared = product(real + imag, table, 0, from_left)
    if conjugate:
        first = product(real, table, 2, from_left)
        second = product(imag, table, 1, from_left)
        return shared + second, shared - first
    first = product(real, table, 1, from_left)
    second = product(imag, table, 2, from_left)
    return shared - second, shared + first


def sandwich(real, imag, table, conjugate):
    real, imag = complex_product(real, imag, table, conjugate, False)
    return complex_product(real, imag, table, conjugate, True)


def block(number):
    return pl.ds(pl.multiple_of(number * HALF, HALF), HALF)


def cut_piece(strip_ref, column, out_ref):
    first = lax.shift_right_logical(column, 7)
    offset = jnp.bitwise_and(column, HALF - 1)
    lanes = lax.broadcasted_iota(jnp.int32, (HALF, HALF), 1)
    mine = lanes >= offset
    third = jnp.minimum(first + 2, strip_ref.shape[-1] // HALF - 1)
    for part in range(2):
        out_ref[part, :, 0:HALF] = jnp.where(
            mine, strip_ref[0, part, :, block(first)], strip_ref[0, part, :, block(third)]
        )
        out_ref[part, :, HALF:WIN] = strip_ref[0, part, :, block(first + 1)]


def cut_partner_kernel(first_ref, second_ref, strip_ref, to_first_ref, to_second_ref):
    for slot in range(2):
        cut_piece(strip_ref, first_ref[slot, 1], to_first_ref.at[slot])
        cut_piece(strip_ref, second_ref[slot, 1], to_second_ref.at[slot])


def cut_own_kernel(pos_ref, strip_ref, after_ref, same_ref, cross_ref):
    core = lax.axis_index("cuts")
    cut_piece(strip_ref, pos_ref[core, 1], same_ref)
    cut_piece(strip_ref, pos_ref[1 - core, 1], cross_ref)


def from_first(pos_ref, slot, shape):
    tile = lax.axis_index("tile")
    odd = jnp.bitwise_and(tile, 1)
    shift_rows = pos_ref[slot, 0] - (tile - 1) * HALF
    rows = lax.broadcasted_iota(jnp.int32, shape, 0)
    sign = 2 * odd - 1
    return sign * (rows - shift_rows) >= 1 - odd


def merge_kernel(pos_ref, first_ref, second_ref, out_ref):
    slot = 1 - lax.axis_index("cuts")
    mask = from_first(pos_ref, slot, (HALF, WIN))
    for part in range(2):
        out_ref[part] = jnp.where(mask, first_ref[slot, part], second_ref[slot, part])


def slot_kernel(
    pos_ref,
    counts_ref,
    probe_ref,
    dft_ref,
    prop_ref,
    own_same_ref,
    own_cross_ref,
    first_ref,
    second_ref,
    rim_cross_ref,
    intensity_ref,
    out_same_ref,
    out_cross_ref,
    object_ref,
    grad_ref,
    measured_ref,
    sem,
):
    core = lax.axis_index("cuts")
    tile = lax.axis_index("tile")
    live = counts_ref[0] > core

    @pl.when(live)
    def _():
        fetch = pltpu.make_async_copy(intensity_ref.at[core], measured_ref, sem)
        fetch.start()
        shift_rows = pos_ref[core, 0] - (tile - 1) * HALF
        shift_cols = jnp.bitwise_and(pos_ref[core, 1], HALF - 1)
        mask = from_first(pos_ref, core, (HALF, WIN))
        for part in range(2):
            object_ref[core, part, 0:HALF] = jnp.where(
                mask, first_ref[core, part], second_ref[core, part]
            )
            object_ref[core, part, HALF:WIN] = own_same_ref[part]
            object_ref[1 - core, part, 0:HALF] = rim_cross_ref[part]
            object_ref[1 - core, part, HALF:WIN] = own_cross_ref[part]

        def rolled(part):
            return pltpu.roll(pltpu.roll(probe_ref[part], shift_rows, 0), shift_cols, 1)

        zero_re, zero_im = rolled(0), rolled(1)
        cell_re, cell_im = object_ref[0, 0], object_ref[0, 1]
        one_re, one_im = sandwich(
            zero_re * cell_re - zero_im * cell_im,
            zero_re * cell_im + zero_im * cell_re,
            prop_ref,
            False,
        )
        cell_re, cell_im = object_ref[1, 0], object_ref[1, 1]
        far_re, far_im = sandwich(
            one_re * cell_re - one_im * cell_im,
            one_re * cell_im + one_im * cell_re,
            dft_ref,
            False,
        )
        fetch.wait()
        residual = far_re * far_re + far_im * far_im - measured_ref[...]
        back_re, back_im = sandwich(far_re * residual, far_im * residual, dft_ref, True)
        grad_ref[1, 0] = one_re * back_re + one_im * back_im
        grad_ref[1, 1] = one_re * back_im - one_im * back_re
        back_re, back_im = sandwich(
            cell_re * back_re + cell_im * back_im,
            cell_re * back_im - cell_im * back_re,
            prop_ref,
            True,
        )
        grad_ref[0, 0] = zero_re * back_re + zero_im * back_im
        grad_ref[0, 1] = zero_re * back_im - zero_im * back_re

    @pl.when(jnp.logical_not(live))
    def _():
        grad_ref[...] = jnp.zeros_like(grad_ref)

    out_same_ref[...] = grad_ref[core]
    out_cross_ref[...] = grad_ref[1 - core]


def pack_kernel(same_ref, cross_ref, out_ref):
    core = lax.axis_index("cuts")
    out_ref[core] = same_ref[:, 0:HALF]
    out_ref[1 - core] = cross_ref[:, 0:HALF]


def add_piece(out_ref, piece_ref, column, keep):
    first = lax.shift_right_logical(column, 7)
    offset = jnp.bitwise_and(column, HALF - 1)
    lanes = lax.broadcasted_iota(jnp.int32, (HALF, HALF), 1)
    mine = lanes >= offset
    third = jnp.minimum(first + 2, out_ref.shape[-1] // HALF - 1)
    for part in range(2):
        left = piece_ref[part, :, 0:HALF]
        right = piece_ref[part, :, HALF:WIN]
        if keep is not None:
            left = jnp.where(keep, left, 0.0)
            right = jnp.where(keep, right, 0.0)
        out_ref[0, part, :, block(first)] += jnp.where(mine, left, 0.0)
        out_ref[0, part, :, block(first + 1)] += right
        out_ref[0, part, :, block(third)] += jnp.where(mine, 0.0, left)


def collect_kernel(
    pos_ref, pos_first_ref, pos_second_ref, same_ref, cross_ref, first_ref, second_ref, out_ref
):
    core = lax.axis_index("cuts")
    tile = lax.axis_index("tile")
    odd = jnp.bitwise_and(tile, 1)
    out_ref[...] = jnp.zeros_like(out_ref)
    add_piece(out_ref, same_ref.at[:, HALF:WIN], pos_ref[core, 1], None)
    add_piece(out_ref, cross_ref.at[:, HALF:WIN], pos_ref[1 - core, 1], None)
    rows = lax.broadcasted_iota(jnp.int32, (HALF, HALF), 0)
    for nearby_ref, piece_ref, above in (
        (pos_first_ref, first_ref, 1 - odd),
        (pos_second_ref, second_ref, odd),
    ):
        sign = 2 * above - 1
        for slot in range(2):
            shift_rows = nearby_ref[slot, 0] - (tile + sign - 1) * HALF
            keep = sign * (rows - shift_rows) >= 1 - above
            add_piece(out_ref, piece_ref.at[slot], nearby_ref[slot, 1], keep)


SMEM = pl.BlockSpec(memory_space=pltpu.SMEM)
VMEM = pl.BlockSpec(memory_space=pltpu.VMEM)
ANY = pl.BlockSpec(memory_space=pl.ANY)


def cost(flops, moved):
    return pl.CostEstimate(flops=flops, bytes_accessed=moved, transcendentals=0)


def local(object_slices, probe, positions, counts, intensity):
    tiles = lax.axis_size("tile")

    def exchange(value, partner):
        pairs = [(core * tiles + tile, core * tiles + partner(tile)) for core in range(2) for tile in range(tiles)]
        pairs = [pair for pair in pairs if pair[1] // tiles == pair[0] // tiles and pair[1] >= 0]
        return lax.ppermute(value, ("cuts", "tile"), pairs)

    def first(value):
        return exchange(value, lambda tile: tile ^ 1)

    def second(value):
        return exchange(value, lambda tile: ((tile + 1) ^ 1) - 1)

    def sibling(value):
        return lax.ppermute(value, "cuts", [(0, 1), (1, 0)])

    def shape(*extent):
        return jax.ShapeDtypeStruct(extent, jnp.float32)

    piece = shape(2, HALF, WIN)
    whole = shape(2, WIN, WIN)
    both = shape(2, 2, HALF, WIN)
    dft, prop = build_tables()
    pos_second = second(positions)
    pos_first = first(positions)
    to_first, to_second = pl.pallas_call(
        cut_partner_kernel,
        out_shape=(both,) * 2,
        in_specs=[SMEM, SMEM, VMEM],
        out_specs=(VMEM,) * 2,
        cost_estimate=cost(0, 3 << 20),
        compiler_params=pltpu.CompilerParams(vmem_limit_bytes=8 << 20),
        name="cut_partner",
    )(pos_first, pos_second, object_slices)
    got_second = second(to_second)
    got_first = first(to_first)
    own_same, to_sibling = pl.pallas_call(
        cut_own_kernel,
        out_shape=(piece,) * 2,
        in_specs=[SMEM, VMEM, ANY],
        out_specs=(VMEM,) * 2,
        cost_estimate=cost(0, 3 << 20),
        compiler_params=pltpu.CompilerParams(vmem_limit_bytes=8 << 20),
        name="cut_own",
    )(positions, object_slices, to_first)
    own_cross = sibling(to_sibling)
    rim_cross = sibling(
        pl.pallas_call(
            merge_kernel,
            out_shape=piece,
            in_specs=[SMEM, VMEM, VMEM],
            out_specs=VMEM,
            cost_estimate=cost(0, 1 << 20),
            compiler_params=pltpu.CompilerParams(vmem_limit_bytes=8 << 20),
        name="merge",
        )(positions, got_first, got_second)
    )
    grad_same, grad_cross = pl.pallas_call(
        slot_kernel,
        out_shape=(whole,) * 2,
        in_specs=[SMEM, SMEM] + [VMEM] * 8 + [ANY],
        out_specs=(VMEM,) * 2,
        scratch_shapes=[
            pltpu.VMEM((2, 2, WIN, WIN), jnp.float32),
            pltpu.VMEM((2, 2, WIN, WIN), jnp.float32),
            pltpu.VMEM((WIN, WIN), jnp.float32),
            pltpu.SemaphoreType.DMA,
        ],
        compiler_params=pltpu.CompilerParams(vmem_limit_bytes=16 << 20),
        cost_estimate=cost(72 * 2 * WIN**3, 6 << 20),
        name="slot",
    )(
        positions,
        counts,
        probe,
        jnp.asarray(dft),
        jnp.asarray(prop),
        own_same,
        own_cross,
        got_first,
        got_second,
        rim_cross,
        intensity,
    )
    grad_cross = sibling(grad_cross)
    rims = pl.pallas_call(
        pack_kernel,
        out_shape=both,
        in_specs=[VMEM, VMEM],
        out_specs=VMEM,
        cost_estimate=cost(0, 1 << 20),
        compiler_params=pltpu.CompilerParams(vmem_limit_bytes=8 << 20),
        name="pack",
    )(grad_same, grad_cross)
    back_second = second(rims)
    back_first = first(rims)
    return pl.pallas_call(
        collect_kernel,
        out_shape=jax.ShapeDtypeStruct(object_slices.shape, jnp.float32),
        in_specs=[SMEM] * 3 + [VMEM] * 4,
        out_specs=VMEM,
        compiler_params=pltpu.CompilerParams(vmem_limit_bytes=16 << 20),
        cost_estimate=cost(0, 4 << 20),
        name="collect",
    )(positions, pos_first, pos_second, grad_same, grad_cross, back_first, back_second)


def solution(mesh):
    in_specs = (
        P("cuts", None, "tile", None),
        P(),
        P("tile", None),
        P("tile"),
        P("tile", None, None),
    )
    out_specs = P("cuts", None, "tile", None)
    return jax.shard_map(local, mesh=mesh, in_specs=in_specs, out_specs=out_specs, check_vma=False)
```

```python
import numpy as np
import ml_dtypes

import jax
import jax.numpy as jnp
from jax import lax
from jax.experimental import pallas as pl
from jax.experimental.pallas import tpu as pltpu
from jax.sharding import PartitionSpec as P

WIN = 256
HALF = 128


def split_tables(real_part, imag_part):
    parts = []
    for values in (real_part, imag_part - real_part, real_part + imag_part):
        high = values.astype(ml_dtypes.bfloat16)
        low = (values - high.astype(np.float64)).astype(ml_dtypes.bfloat16)
        parts += [high, low]
    return np.stack(parts)


def build_tables():
    index = np.arange(WIN)
    turned = 2.0 * np.pi * ((index[:, None] * index[None, :]) % WIN) / WIN
    dft = (np.cos(turned) - 1j * np.sin(turned)) / np.sqrt(WIN)
    centred = (index + WIN // 2) % WIN - WIN // 2
    phase = np.pi * (centred * centred % (4 * WIN)) / (2 * WIN)
    prop = np.conj(dft) @ ((np.cos(phase) - 1j * np.sin(phase))[:, None] * dft)
    prop = 0.5 * (prop + prop.T)
    return split_tables(dft.real, dft.imag), split_tables(prop.real, prop.imag)


def split(value):
    high = value.astype(jnp.bfloat16)
    low = (value - high.astype(jnp.float32)).astype(jnp.bfloat16)
    return high, low


def dot(left, right):
    return jnp.dot(left, right, preferred_element_type=jnp.float32)


def product(field, table, which, from_left):
    high, low = split(field)
    table_high = table[2 * which]
    table_low = table[2 * which + 1]
    if from_left:
        return dot(table_high, high) + (dot(table_high, low) + dot(table_low, high))
    return dot(high, table_high) + (dot(low, table_high) + dot(high, table_low))


def complex_product(real, imag, table, conjugate, from_left):
    shared = product(real + imag, table, 0, from_left)
    if conjugate:
        first = product(real, table, 2, from_left)
        second = product(imag, table, 1, from_left)
        return shared + second, shared - first
    first = product(real, table, 1, from_left)
    second = product(imag, table, 2, from_left)
    return shared - second, shared + first


def sandwich(real, imag, table, conjugate):
    real, imag = complex_product(real, imag, table, conjugate, False)
    return complex_product(real, imag, table, conjugate, True)


def block(number):
    return pl.ds(pl.multiple_of(number * HALF, HALF), HALF)


def cut_piece(strip_ref, column, out_ref):
    first = lax.shift_right_logical(column, 7)
    offset = jnp.bitwise_and(column, HALF - 1)
    lanes = lax.broadcasted_iota(jnp.int32, (HALF, HALF), 1)
    mine = lanes >= offset
    third = jnp.minimum(first + 2, strip_ref.shape[-1] // HALF - 1)
    for part in range(2):
        out_ref[part, :, 0:HALF] = jnp.where(
            mine, strip_ref[0, part, :, block(first)], strip_ref[0, part, :, block(third)]
        )
        out_ref[part, :, HALF:WIN] = strip_ref[0, part, :, block(first + 1)]


def cut_kernel(
    below_ref, above_ref, own_ref, other_ref, up_zero_ref, down_zero_ref, up_one_ref, down_one_ref
):
    @pl.when(lax.axis_index("cuts") == 1)
    def _():
        for slot in range(2):
            cut_piece(other_ref, above_ref[slot, 1], up_zero_ref.at[slot])
            cut_piece(other_ref, below_ref[slot, 1], down_zero_ref.at[slot])
        for slot in range(2):
            cut_piece(own_ref, above_ref[slot, 1], up_one_ref.at[slot])
            cut_piece(own_ref, below_ref[slot, 1], down_one_ref.at[slot])


def slot_kernel(
    pos_ref,
    counts_ref,
    probe_ref,
    dft_ref,
    prop_ref,
    own_ref,
    other_ref,
    low_zero_ref,
    high_zero_ref,
    low_one_ref,
    high_one_ref,
    intensity_ref,
    rim_zero_ref,
    rim_one_ref,
    mid_zero_ref,
    mid_one_ref,
    object_ref,
):
    tile = lax.axis_index("tile")
    live_slots = jnp.where(lax.axis_index("cuts") == 0, counts_ref[0], 0)

    @pl.loop(0, live_slots)
    def _(slot):
        shift_rows = pos_ref[slot, 0] - (tile - 1) * HALF
        column = pos_ref[slot, 1]
        shift_cols = jnp.bitwise_and(column, HALF - 1)
        from_low = lax.broadcasted_iota(jnp.int32, (HALF, WIN), 0) >= shift_rows
        for layer, (strip_ref, low_ref, high_ref) in enumerate(
            ((own_ref, low_zero_ref, high_zero_ref), (other_ref, low_one_ref, high_one_ref))
        ):
            for part in range(2):
                object_ref[layer, part, 0:HALF] = jnp.where(
                    from_low, low_ref[slot, part], high_ref[slot, part]
                )
            cut_piece(strip_ref, column, object_ref.at[layer, :, HALF:WIN])

        def rolled(part):
            return pltpu.roll(pltpu.roll(probe_ref[part], shift_rows, 0), shift_cols, 1)

        zero_re, zero_im = rolled(0), rolled(1)
        cell_re, cell_im = object_ref[0, 0], object_ref[0, 1]
        one_re, one_im = sandwich(
            zero_re * cell_re - zero_im * cell_im,
            zero_re * cell_im + zero_im * cell_re,
            prop_ref,
            False,
        )
        cell_re, cell_im = object_ref[1, 0], object_ref[1, 1]
        far_re, far_im = sandwich(
            one_re * cell_re - one_im * cell_im,
            one_re * cell_im + one_im * cell_re,
            dft_ref,
            False,
        )
        residual = far_re * far_re + far_im * far_im - intensity_ref[slot]
        back_re, back_im = sandwich(far_re * residual, far_im * residual, dft_ref, True)
        for part, value in (
            (0, one_re * back_re + one_im * back_im),
            (1, one_re * back_im - one_im * back_re),
        ):
            rim_one_ref[slot, part] = value[0:HALF]
            mid_one_ref[slot, part] = value[HALF:WIN]
        back_re, back_im = sandwich(
            cell_re * back_re + cell_im * back_im,
            cell_re * back_im - cell_im * back_re,
            prop_ref,
            True,
        )
        for part, value in (
            (0, zero_re * back_re + zero_im * back_im),
            (1, zero_re * back_im - zero_im * back_re),
        ):
            rim_zero_ref[slot, part] = value[0:HALF]
            mid_zero_ref[slot, part] = value[HALF:WIN]

    @pl.when(live_slots == 1)
    def _():
        for ref in (rim_zero_ref, rim_one_ref, mid_zero_ref, mid_one_ref):
            ref[1] = jnp.zeros_like(ref[1])


def add_piece(out_ref, piece_ref, column, keep):
    first = lax.shift_right_logical(column, 7)
    offset = jnp.bitwise_and(column, HALF - 1)
    lanes = lax.broadcasted_iota(jnp.int32, (HALF, HALF), 1)
    mine = lanes >= offset
    third = jnp.minimum(first + 2, out_ref.shape[-1] // HALF - 1)
    for part in range(2):
        left = piece_ref[part, :, 0:HALF]
        right = piece_ref[part, :, HALF:WIN]
        if keep is not None:
            left = jnp.where(keep, left, 0.0)
            right = jnp.where(keep, right, 0.0)
        out_ref[0, part, :, block(first)] += jnp.where(mine, left, 0.0)
        out_ref[0, part, :, block(first + 1)] += right
        out_ref[0, part, :, block(third)] += jnp.where(mine, 0.0, left)


def collect_kernel(
    pos_ref,
    below_ref,
    above_ref,
    below_copy_ref,
    above_copy_ref,
    mid_zero_ref,
    up_zero_ref,
    down_zero_ref,
    mid_one_ref,
    up_one_ref,
    down_one_ref,
    out_ref,
):
    core = lax.axis_index("cuts")
    tile = lax.axis_index("tile")
    out_ref[...] = jnp.zeros_like(out_ref)
    rows = lax.broadcasted_iota(jnp.int32, (HALF, HALF), 0)

    def gather(lower_ref, upper_ref, mid_ref, up_ref, down_ref):
        for slot in range(2):
            add_piece(out_ref, mid_ref.at[slot], pos_ref[slot, 1], None)
            keep = rows < lower_ref[slot, 0] - (tile - 2) * HALF
            add_piece(out_ref, up_ref.at[slot], lower_ref[slot, 1], keep)
            keep = rows >= upper_ref[slot, 0] - tile * HALF
            add_piece(out_ref, down_ref.at[slot], upper_ref[slot, 1], keep)

    @pl.when(core == 0)
    def _():
        gather(below_copy_ref, above_copy_ref, mid_zero_ref, up_zero_ref, down_zero_ref)

    @pl.when(core == 1)
    def _():
        gather(below_ref, above_ref, mid_one_ref, up_one_ref, down_one_ref)


SMEM = pl.BlockSpec(memory_space=pltpu.SMEM)
VMEM = pl.BlockSpec(memory_space=pltpu.VMEM)
ANY = pl.BlockSpec(memory_space=pl.ANY)


LIMIT = 12 << 20


def local(object_slices, probe, positions, counts, intensity):
    tiles = lax.axis_size("tile")

    def send(value, source, target, by):
        pairs = []
        for tile in range(tiles):
            if 0 <= tile + by < tiles:
                pairs.append((source * tiles + tile, target * tiles + tile + by))
        return lax.ppermute(value, ("cuts", "tile"), pairs)

    def kernel(body, name, out_shape, in_specs, flops, moved, scratch=(), out_specs=None):
        return pl.pallas_call(
            body,
            out_shape=out_shape,
            in_specs=in_specs,
            out_specs=VMEM if out_specs is None else out_specs,
            scratch_shapes=scratch,
            compiler_params=pltpu.CompilerParams(vmem_limit_bytes=LIMIT),
            cost_estimate=pl.CostEstimate(flops=flops, bytes_accessed=moved, transcendentals=0),
            name=name,
        )

    pieces = jax.ShapeDtypeStruct((2, 2, HALF, WIN), jnp.float32)
    dft, prop = build_tables()
    other_slice = lax.ppermute(object_slices, "cuts", [(0, 1), (1, 0)])
    below = send(positions, 0, 1, 1)
    above = send(positions, 0, 1, -1)
    up_zero, down_zero, up_one, down_one = kernel(
        cut_kernel, "cut", (pieces,) * 4, [SMEM] * 2 + [VMEM] * 2, 0, 4 << 20, (), (VMEM,) * 4
    )(below, above, object_slices, other_slice)
    low_zero = send(up_zero, 1, 0, 1)
    high_zero = send(down_zero, 1, 0, -1)
    low_one = send(up_one, 1, 0, 1)
    high_one = send(down_one, 1, 0, -1)
    below_copy = send(below, 1, 0, 0)
    above_copy = send(above, 1, 0, 0)
    rim_zero, rim_one, mid_zero, mid_one = kernel(
        slot_kernel,
        "slot",
        (pieces,) * 4,
        [SMEM] * 2 + [VMEM] * 10,
        72 * 2 * WIN**3,
        6 << 20,
        (pltpu.VMEM((2, 2, WIN, WIN), jnp.float32),),
        (VMEM,) * 4,
    )(
        positions,
        counts,
        probe,
        jnp.asarray(dft),
        jnp.asarray(prop),
        object_slices,
        other_slice,
        low_zero,
        high_zero,
        low_one,
        high_one,
        intensity,
    )
    back_up_one = send(rim_one, 0, 1, 1)
    back_down_one = send(rim_one, 0, 1, -1)
    back_up_zero = send(rim_zero, 0, 0, 1)
    back_down_zero = send(rim_zero, 0, 0, -1)
    mid_one = send(mid_one, 0, 1, 0)
    return kernel(
        collect_kernel,
        "collect",
        jax.ShapeDtypeStruct(object_slices.shape, jnp.float32),
        [SMEM] * 5 + [VMEM] * 6,
        0,
        4 << 20,
    )(
        positions,
        below,
        above,
        below_copy,
        above_copy,
        mid_zero,
        back_up_zero,
        back_down_zero,
        mid_one,
        back_up_one,
        back_down_one,
    )


def solution(mesh):
    in_specs = (
        P("cuts", None, "tile", None),
        P(),
        P("tile", None),
        P("tile"),
        P("tile", None, None),
    )
    out_specs = P("cuts", None, "tile", None)
    return jax.shard_map(local, mesh=mesh, in_specs=in_specs, out_specs=out_specs, check_vma=False)
```

```python
import numpy as np
import ml_dtypes

import jax
import jax.numpy as jnp
from jax import lax
from jax.experimental import pallas as pl
from jax.experimental.pallas import tpu as pltpu
from jax.sharding import PartitionSpec as P

WIN = 256
HALF = 128


def split_tables(real_part, imag_part):
    parts = []
    for values in (real_part, imag_part - real_part, real_part + imag_part):
        high = values.astype(ml_dtypes.bfloat16)
        low = (values - high.astype(np.float64)).astype(ml_dtypes.bfloat16)
        parts += [high, low]
    return np.stack(parts)


def build_tables():
    index = np.arange(WIN)
    turned = 2.0 * np.pi * ((index[:, None] * index[None, :]) % WIN) / WIN
    dft = (np.cos(turned) - 1j * np.sin(turned)) / np.sqrt(WIN)
    centred = (index + WIN // 2) % WIN - WIN // 2
    phase = np.pi * (centred * centred % (4 * WIN)) / (2 * WIN)
    prop = np.conj(dft) @ ((np.cos(phase) - 1j * np.sin(phase))[:, None] * dft)
    prop = 0.5 * (prop + prop.T)
    return split_tables(dft.real, dft.imag), split_tables(prop.real, prop.imag)


def split(value):
    high = value.astype(jnp.bfloat16)
    low = (value - high.astype(jnp.float32)).astype(jnp.bfloat16)
    return high, low


def dot(left, right):
    return jnp.dot(left, right, preferred_element_type=jnp.float32)


def product(field, table, which, from_left):
    high, low = split(field)
    table_high = table[2 * which]
    table_low = table[2 * which + 1]
    if from_left:
        return dot(table_high, high) + (dot(table_high, low) + dot(table_low, high))
    return dot(high, table_high) + (dot(low, table_high) + dot(high, table_low))


def complex_product(real, imag, table, conjugate, from_left):
    shared = product(real + imag, table, 0, from_left)
    if conjugate:
        first = product(real, table, 2, from_left)
        second = product(imag, table, 1, from_left)
        return shared + second, shared - first
    first = product(real, table, 1, from_left)
    second = product(imag, table, 2, from_left)
    return shared - second, shared + first


def sandwich(real, imag, table, conjugate):
    real, imag = complex_product(real, imag, table, conjugate, False)
    return complex_product(real, imag, table, conjugate, True)


def block(number):
    return pl.ds(pl.multiple_of(number * HALF, HALF), HALF)


def cut_piece(strip_ref, column, out_ref):
    first = lax.shift_right_logical(column, 7)
    offset = jnp.bitwise_and(column, HALF - 1)
    lanes = lax.broadcasted_iota(jnp.int32, (HALF, HALF), 1)
    mine = lanes >= offset
    third = jnp.minimum(first + 2, strip_ref.shape[-1] // HALF - 1)
    for part in range(2):
        out_ref[part, :, 0:HALF] = jnp.where(
            mine, strip_ref[0, part, :, block(first)], strip_ref[0, part, :, block(third)]
        )
        out_ref[part, :, HALF:WIN] = strip_ref[0, part, :, block(first + 1)]


def stage_kernel(strip_ref, out_ref, sem):
    copy = pltpu.make_async_copy(strip_ref, out_ref, sem)
    copy.start()
    copy.wait()


def is_odd():
    return jnp.bitwise_and(lax.axis_index("tile"), 1)


def cut_kernel(
    first_ref, second_ref, own_ref, other_ref, up_zero_ref, down_zero_ref, up_one_ref, down_one_ref
):
    @pl.when(lax.axis_index("cuts") == 1)
    def _():
        odd = is_odd() == 1
        for strip_ref, up_ref, down_ref in (
            (other_ref, up_zero_ref, down_zero_ref),
            (own_ref, up_one_ref, down_one_ref),
        ):
            for slot in range(2):
                first, second = first_ref[slot, 1], second_ref[slot, 1]
                cut_piece(strip_ref, jnp.where(odd, second, first), up_ref.at[slot])
                cut_piece(strip_ref, jnp.where(odd, first, second), down_ref.at[slot])


def slots_of_core(counts_ref):
    return jnp.where(lax.axis_index("cuts") == 0, counts_ref[0], 0)


def fill_window(pos_ref, slot, strip_ref, low_ref, high_ref, window_ref):
    shift_rows = pos_ref[slot, 0] - (lax.axis_index("tile") - 1) * HALF
    column = pos_ref[slot, 1]
    from_low = lax.broadcasted_iota(jnp.int32, (HALF, WIN), 0) >= shift_rows
    for part in range(2):
        window_ref[part, 0:HALF] = jnp.where(from_low, low_ref[slot, part], high_ref[slot, part])
    cut_piece(strip_ref, column, window_ref.at[:, HALF:WIN])
    return shift_rows, jnp.bitwise_and(column, HALF - 1)


def enter_kernel(
    pos_ref, counts_ref, probe_ref, table_ref, own_ref, low_ref, high_ref, wave_ref, window_ref
):
    @pl.loop(0, slots_of_core(counts_ref))
    def _(slot):
        shift_rows, shift_cols = fill_window(pos_ref, slot, own_ref, low_ref, high_ref, window_ref)

        def rolled(part):
            return pltpu.roll(pltpu.roll(probe_ref[part], shift_rows, 0), shift_cols, 1)

        zero_re, zero_im = rolled(0), rolled(1)
        wave_ref[slot, 0, 0] = zero_re
        wave_ref[slot, 0, 1] = zero_im
        cell_re, cell_im = window_ref[0], window_ref[1]
        one_re, one_im = sandwich(
            zero_re * cell_re - zero_im * cell_im,
            zero_re * cell_im + zero_im * cell_re,
            table_ref.at[1],
            False,
        )
        wave_ref[slot, 1, 0] = one_re
        wave_ref[slot, 1, 1] = one_im


def slot_kernel(
    pos_ref,
    counts_ref,
    table_ref,
    wave_ref,
    other_ref,
    low_ref,
    high_ref,
    intensity_ref,
    rim_zero_ref,
    rim_one_ref,
    mid_zero_ref,
    mid_one_ref,
    window_ref,
):
    live_slots = slots_of_core(counts_ref)
    dft_ref, prop_ref = table_ref.at[0], table_ref.at[1]

    @pl.loop(0, live_slots)
    def _(slot):
        fill_window(pos_ref, slot, other_ref, low_ref, high_ref, window_ref)
        cell_re, cell_im = window_ref[0], window_ref[1]
        one_re, one_im = wave_ref[slot, 1, 0], wave_ref[slot, 1, 1]
        far_re, far_im = sandwich(
            one_re * cell_re - one_im * cell_im,
            one_re * cell_im + one_im * cell_re,
            dft_ref,
            False,
        )
        residual = far_re * far_re + far_im * far_im - intensity_ref[slot]
        back_re, back_im = sandwich(far_re * residual, far_im * residual, dft_ref, True)
        for part, value in (
            (0, one_re * back_re + one_im * back_im),
            (1, one_re * back_im - one_im * back_re),
        ):
            rim_one_ref[slot, part] = value[0:HALF]
            mid_one_ref[slot, part] = value[HALF:WIN]
        back_re, back_im = sandwich(
            cell_re * back_re + cell_im * back_im,
            cell_re * back_im - cell_im * back_re,
            prop_ref,
            True,
        )
        zero_re, zero_im = wave_ref[slot, 0, 0], wave_ref[slot, 0, 1]
        for part, value in (
            (0, zero_re * back_re + zero_im * back_im),
            (1, zero_re * back_im - zero_im * back_re),
        ):
            rim_zero_ref[slot, part] = value[0:HALF]
            mid_zero_ref[slot, part] = value[HALF:WIN]

    @pl.when(live_slots == 1)
    def _():
        for ref in (rim_zero_ref, rim_one_ref, mid_zero_ref, mid_one_ref):
            ref[1] = jnp.zeros_like(ref[1])


def add_piece(out_ref, piece_ref, column, keep):
    first = lax.shift_right_logical(column, 7)
    offset = jnp.bitwise_and(column, HALF - 1)
    lanes = lax.broadcasted_iota(jnp.int32, (HALF, HALF), 1)
    mine = lanes >= offset
    third = jnp.minimum(first + 2, out_ref.shape[-1] // HALF - 1)
    for part in range(2):
        left = piece_ref[part, :, 0:HALF]
        right = piece_ref[part, :, HALF:WIN]
        if keep is not None:
            left = jnp.where(keep, left, 0.0)
            right = jnp.where(keep, right, 0.0)
        out_ref[0, part, :, block(first)] += jnp.where(mine, left, 0.0)
        out_ref[0, part, :, block(first + 1)] += right
        out_ref[0, part, :, block(third)] += jnp.where(mine, 0.0, left)


def collect_kernel(
    pos_ref,
    first_ref,
    second_ref,
    first_copy_ref,
    second_copy_ref,
    mid_zero_ref,
    first_zero_ref,
    second_zero_ref,
    mid_one_ref,
    up_one_ref,
    down_one_ref,
    out_ref,
):
    core = lax.axis_index("cuts")
    tile = lax.axis_index("tile")
    odd = is_odd()
    out_ref[...] = jnp.zeros_like(out_ref)
    rows = lax.broadcasted_iota(jnp.int32, (HALF, HALF), 0)

    def add(piece_ref, slot, row, column, above):
        sign = 2 * above - 1
        keep = sign * (rows - (row - (tile + sign - 1) * HALF)) >= 1 - above
        add_piece(out_ref, piece_ref.at[slot], column, keep)

    @pl.when(core == 0)
    def _():
        for slot in range(2):
            add_piece(out_ref, mid_zero_ref.at[slot], pos_ref[slot, 1], None)
            row, column = first_copy_ref[slot, 0], first_copy_ref[slot, 1]
            add(first_zero_ref, slot, row, column, 1 - odd)
            row, column = second_copy_ref[slot, 0], second_copy_ref[slot, 1]
            add(second_zero_ref, slot, row, column, odd)

    @pl.when(core == 1)
    def _():
        for slot in range(2):
            add_piece(out_ref, mid_one_ref.at[slot], pos_ref[slot, 1], None)
            first = first_ref[slot, 0], first_ref[slot, 1]
            second = second_ref[slot, 0], second_ref[slot, 1]
            below = [jnp.where(odd == 1, one, two) for one, two in zip(first, second)]
            above = [jnp.where(odd == 1, two, one) for one, two in zip(first, second)]
            add(up_one_ref, slot, *below, 0)
            add(down_one_ref, slot, *above, 1)


SMEM = pl.BlockSpec(memory_space=pltpu.SMEM)
VMEM = pl.BlockSpec(memory_space=pltpu.VMEM)
ANY = pl.BlockSpec(memory_space=pl.ANY)


LIMIT = 12 << 20


def local(object_slices, probe, positions, counts, intensity):
    tiles = lax.axis_size("tile")

    def send(value, source, target, by):
        pairs = []
        for tile in range(tiles):
            if 0 <= tile + by < tiles:
                pairs.append((source * tiles + tile, target * tiles + tile + by))
        return lax.ppermute(value, ("cuts", "tile"), pairs)

    def swap(value, cores, partner):
        pairs = [(tile, partner(tile)) for tile in range(tiles) if 0 <= partner(tile) < tiles]
        pairs = [(core * tiles + one, core * tiles + two) for core in cores for one, two in pairs]
        return lax.ppermute(value, ("cuts", "tile"), pairs)

    def first(tile):
        return tile ^ 1

    def second(tile):
        return ((tile + 1) ^ 1) - 1

    def kernel(body, name, out_shape, in_specs, flops, moved, scratch=(), out_specs=None):
        return pl.pallas_call(
            body,
            out_shape=out_shape,
            in_specs=in_specs,
            out_specs=VMEM if out_specs is None else out_specs,
            scratch_shapes=scratch,
            compiler_params=pltpu.CompilerParams(vmem_limit_bytes=LIMIT),
            cost_estimate=pl.CostEstimate(flops=flops, bytes_accessed=moved, transcendentals=0),
            name=name,
        )

    pieces = jax.ShapeDtypeStruct((2, 2, HALF, WIN), jnp.float32)
    tables = jnp.asarray(np.stack(build_tables()))
    other_slice = lax.ppermute(object_slices, "cuts", [(0, 1), (1, 0)])
    pos_second = swap(positions, (1,), second)
    pos_first = swap(positions, (1,), first)
    strip = jax.ShapeDtypeStruct(object_slices.shape, jnp.float32)
    own_slice = kernel(
        stage_kernel, "stage", strip, [ANY], 0, 4 << 20, (pltpu.SemaphoreType.DMA,)
    )(object_slices)
    up_zero, down_zero, up_one, down_one = kernel(
        cut_kernel, "cut", (pieces,) * 4, [SMEM] * 2 + [VMEM] * 2, 0, 4 << 20, (), (VMEM,) * 4
    )(pos_first, pos_second, own_slice, other_slice)
    low_zero = send(up_zero, 1, 0, 1)
    high_zero = send(down_zero, 1, 0, -1)
    low_one = send(up_one, 1, 0, 1)
    high_one = send(down_one, 1, 0, -1)
    second_copy = send(pos_second, 1, 0, 0)
    first_copy = send(pos_first, 1, 0, 0)
    window = (pltpu.VMEM((2, WIN, WIN), jnp.float32),)
    wave = kernel(
        enter_kernel,
        "enter",
        jax.ShapeDtypeStruct((2, 2, 2, WIN, WIN), jnp.float32),
        [SMEM] * 2 + [VMEM] * 5,
        18 * 2 * WIN**3,
        3 << 20,
        window,
    )(positions, counts, probe, tables, own_slice, low_zero, high_zero)
    rim_zero, rim_one, mid_zero, mid_one = kernel(
        slot_kernel,
        "slot",
        (pieces,) * 4,
        [SMEM] * 2 + [VMEM] * 6,
        54 * 2 * WIN**3,
        6 << 20,
        window,
        (VMEM,) * 4,
    )(positions, counts, tables, wave, other_slice, low_one, high_one, intensity)
    back_up_one = send(rim_one, 0, 1, 1)
    back_down_one = send(rim_one, 0, 1, -1)
    back_second = swap(rim_zero, (0,), second)
    back_first = swap(rim_zero, (0,), first)
    mid_one = send(mid_one, 0, 1, 0)
    return kernel(collect_kernel, "collect", strip, [SMEM] * 5 + [VMEM] * 6, 0, 4 << 20)(
        positions,
        pos_first,
        pos_second,
        first_copy,
        second_copy,
        mid_zero,
        back_first,
        back_second,
        mid_one,
        back_up_one,
        back_down_one,
    )


def solution(mesh):
    in_specs = (
        P("cuts", None, "tile", None),
        P(),
        P("tile", None),
        P("tile"),
        P("tile", None, None),
    )
    out_specs = P("cuts", None, "tile", None)
    return jax.shard_map(local, mesh=mesh, in_specs=in_specs, out_specs=out_specs, check_vma=False)
```

```python
import numpy as np
import ml_dtypes

import jax
import jax.numpy as jnp
from jax import lax
from jax.experimental import pallas as pl
from jax.experimental.pallas import tpu as pltpu
from jax.sharding import PartitionSpec as P

WIN = 256
HALF = 128


def split_tables(real_part, imag_part):
    parts = []
    for values in (real_part, imag_part - real_part, real_part + imag_part):
        high = values.astype(ml_dtypes.bfloat16)
        low = (values - high.astype(np.float64)).astype(ml_dtypes.bfloat16)
        parts += [high, low]
    return np.stack(parts)


def build_tables():
    index = np.arange(WIN)
    turned = 2.0 * np.pi * ((index[:, None] * index[None, :]) % WIN) / WIN
    dft = (np.cos(turned) - 1j * np.sin(turned)) / np.sqrt(WIN)
    centred = (index + WIN // 2) % WIN - WIN // 2
    phase = np.pi * (centred * centred % (4 * WIN)) / (2 * WIN)
    prop = np.conj(dft) @ ((np.cos(phase) - 1j * np.sin(phase))[:, None] * dft)
    prop = 0.5 * (prop + prop.T)
    return split_tables(dft.real, dft.imag), split_tables(prop.real, prop.imag)


def split(value):
    high = value.astype(jnp.bfloat16)
    low = (value - high.astype(jnp.float32)).astype(jnp.bfloat16)
    return high, low


def dot(left, right):
    return jnp.dot(left, right, preferred_element_type=jnp.float32)


def product(field, table, which, from_left):
    high, low = split(field)
    table_high = table[2 * which]
    table_low = table[2 * which + 1]
    if from_left:
        return dot(table_high, high) + (dot(table_high, low) + dot(table_low, high))
    return dot(high, table_high) + (dot(low, table_high) + dot(high, table_low))


def complex_product(real, imag, table, conjugate, from_left):
    shared = product(real + imag, table, 0, from_left)
    if conjugate:
        first = product(real, table, 2, from_left)
        second = product(imag, table, 1, from_left)
        return shared + second, shared - first
    first = product(real, table, 1, from_left)
    second = product(imag, table, 2, from_left)
    return shared - second, shared + first


def sandwich(real, imag, table, conjugate):
    real, imag = complex_product(real, imag, table, conjugate, False)
    return complex_product(real, imag, table, conjugate, True)


def block(number):
    return pl.ds(pl.multiple_of(number * HALF, HALF), HALF)


def cut_piece(strip_ref, column, out_ref):
    first = lax.shift_right_logical(column, 7)
    offset = jnp.bitwise_and(column, HALF - 1)
    lanes = lax.broadcasted_iota(jnp.int32, (HALF, HALF), 1)
    mine = lanes >= offset
    third = jnp.minimum(first + 2, strip_ref.shape[-1] // HALF - 1)
    for part in range(2):
        out_ref[part, :, 0:HALF] = jnp.where(
            mine, strip_ref[0, part, :, block(first)], strip_ref[0, part, :, block(third)]
        )
        out_ref[part, :, HALF:WIN] = strip_ref[0, part, :, block(first + 1)]


def stage_kernel(pos_ref, strip_ref, pos_out_ref, out_ref, sem):
    copy = pltpu.make_async_copy(strip_ref, out_ref, sem)
    copy.start()
    for slot in range(2):
        for entry in range(2):
            pos_out_ref[slot, entry] = pos_ref[slot, entry]
    copy.wait()


def cut_kernel(pos_ref, strip_ref, after_ref, out_ref):
    @pl.when(lax.axis_index("cuts") == 1)
    def _():
        for slot in range(2):
            cut_piece(strip_ref, pos_ref[slot, 1], out_ref.at[slot])


def slots_of_core(counts_ref):
    return jnp.where(lax.axis_index("cuts") == 0, counts_ref[0], 0)


def fill_window(pos_ref, slot, strip_ref, first_ref, second_ref, window_ref):
    tile = lax.axis_index("tile")
    odd = jnp.bitwise_and(tile, 1)
    shift_rows = pos_ref[slot, 0] - (tile - 1) * HALF
    column = pos_ref[slot, 1]
    rows = lax.broadcasted_iota(jnp.int32, (HALF, WIN), 0)
    from_first = (2 * odd - 1) * (rows - shift_rows) >= 1 - odd
    for part in range(2):
        window_ref[part, 0:HALF] = jnp.where(
            from_first, first_ref[slot, part], second_ref[slot, part]
        )
    cut_piece(strip_ref, column, window_ref.at[:, HALF:WIN])
    return shift_rows, jnp.bitwise_and(column, HALF - 1)


def enter_kernel(
    pos_ref,
    counts_ref,
    probe_ref,
    table_ref,
    own_ref,
    second_ref,
    first_ref,
    second_copy_ref,
    first_copy_ref,
    wave_ref,
    window_ref,
):
    @pl.loop(0, slots_of_core(counts_ref))
    def _(slot):
        shift_rows, shift_cols = fill_window(pos_ref, slot, own_ref, first_ref, second_ref, window_ref)

        def rolled(part):
            return pltpu.roll(pltpu.roll(probe_ref[part], shift_rows, 0), shift_cols, 1)

        zero_re, zero_im = rolled(0), rolled(1)
        wave_ref[slot, 0, 0] = zero_re
        wave_ref[slot, 0, 1] = zero_im
        cell_re, cell_im = window_ref[0], window_ref[1]
        one_re, one_im = sandwich(
            zero_re * cell_re - zero_im * cell_im,
            zero_re * cell_im + zero_im * cell_re,
            table_ref.at[1],
            False,
        )
        wave_ref[slot, 1, 0] = one_re
        wave_ref[slot, 1, 1] = one_im


def slot_kernel(
    pos_ref,
    counts_ref,
    table_ref,
    wave_ref,
    other_ref,
    second_ref,
    first_ref,
    intensity_ref,
    rim_zero_ref,
    rim_one_ref,
    mid_zero_ref,
    mid_one_ref,
    window_ref,
):
    live_slots = slots_of_core(counts_ref)
    dft_ref, prop_ref = table_ref.at[0], table_ref.at[1]

    @pl.loop(0, live_slots)
    def _(slot):
        fill_window(pos_ref, slot, other_ref, first_ref, second_ref, window_ref)
        cell_re, cell_im = window_ref[0], window_ref[1]
        one_re, one_im = wave_ref[slot, 1, 0], wave_ref[slot, 1, 1]
        far_re, far_im = sandwich(
            one_re * cell_re - one_im * cell_im,
            one_re * cell_im + one_im * cell_re,
            dft_ref,
            False,
        )
        residual = far_re * far_re + far_im * far_im - intensity_ref[slot]
        back_re, back_im = sandwich(far_re * residual, far_im * residual, dft_ref, True)
        for part, value in (
            (0, one_re * back_re + one_im * back_im),
            (1, one_re * back_im - one_im * back_re),
        ):
            rim_one_ref[slot, part] = value[0:HALF]
            mid_one_ref[slot, part] = value[HALF:WIN]
        back_re, back_im = sandwich(
            cell_re * back_re + cell_im * back_im,
            cell_re * back_im - cell_im * back_re,
            prop_ref,
            True,
        )
        zero_re, zero_im = wave_ref[slot, 0, 0], wave_ref[slot, 0, 1]
        for part, value in (
            (0, zero_re * back_re + zero_im * back_im),
            (1, zero_re * back_im - zero_im * back_re),
        ):
            rim_zero_ref[slot, part] = value[0:HALF]
            mid_zero_ref[slot, part] = value[HALF:WIN]

    @pl.when(live_slots == 1)
    def _():
        for ref in (rim_zero_ref, rim_one_ref, mid_zero_ref, mid_one_ref):
            ref[1] = jnp.zeros_like(ref[1])


def add_piece(out_ref, piece_ref, column, keep):
    first = lax.shift_right_logical(column, 7)
    offset = jnp.bitwise_and(column, HALF - 1)
    lanes = lax.broadcasted_iota(jnp.int32, (HALF, HALF), 1)
    mine = lanes >= offset
    third = jnp.minimum(first + 2, out_ref.shape[-1] // HALF - 1)
    for part in range(2):
        left = piece_ref[part, :, 0:HALF]
        right = piece_ref[part, :, HALF:WIN]
        if keep is not None:
            left = jnp.where(keep, left, 0.0)
            right = jnp.where(keep, right, 0.0)
        out_ref[0, part, :, block(first)] += jnp.where(mine, left, 0.0)
        out_ref[0, part, :, block(first + 1)] += right
        out_ref[0, part, :, block(third)] += jnp.where(mine, 0.0, left)


def collect_kernel(
    pos_ref,
    second_ref,
    first_ref,
    second_copy_ref,
    first_copy_ref,
    mid_zero_ref,
    second_zero_ref,
    first_zero_ref,
    second_one_ref,
    first_one_ref,
    mid_one_ref,
    out_ref,
):
    core = lax.axis_index("cuts")
    tile = lax.axis_index("tile")
    odd = jnp.bitwise_and(tile, 1)
    out_ref[...] = jnp.zeros_like(out_ref)
    rows = lax.broadcasted_iota(jnp.int32, (HALF, HALF), 0)

    def gather(mid_ref, *nearby):
        for slot in range(2):
            add_piece(out_ref, mid_ref.at[slot], pos_ref[slot, 1], None)
        for piece_ref, place_ref, above in nearby:
            sign = 2 * above - 1
            for slot in range(2):
                shift_rows = place_ref[slot, 0] - (tile + sign - 1) * HALF
                keep = sign * (rows - shift_rows) >= 1 - above
                add_piece(out_ref, piece_ref.at[slot], place_ref[slot, 1], keep)

    @pl.when(core == 0)
    def _():
        gather(
            mid_zero_ref,
            (second_zero_ref, second_copy_ref, odd),
            (first_zero_ref, first_copy_ref, 1 - odd),
        )

    @pl.when(core == 1)
    def _():
        gather(
            mid_one_ref,
            (second_one_ref, second_ref, odd),
            (first_one_ref, first_ref, 1 - odd),
        )


SMEM = pl.BlockSpec(memory_space=pltpu.SMEM)
VMEM = pl.BlockSpec(memory_space=pltpu.VMEM)
ANY = pl.BlockSpec(memory_space=pl.ANY)


LIMIT = 12 << 20


def local(object_slices, probe, positions, counts, intensity):
    tiles = lax.axis_size("tile")

    def first(tile):
        return tile ^ 1

    def second(tile):
        return ((tile + 1) ^ 1) - 1

    def same(tile):
        return tile

    def send(value, source, target, partner):
        pairs = [(tile, partner(tile)) for tile in range(tiles) if 0 <= partner(tile) < tiles]
        pairs = [(source * tiles + one, target * tiles + two) for one, two in pairs]
        return lax.ppermute(value, ("cuts", "tile"), pairs)

    def kernel(body, name, out_shape, in_specs, flops, moved, scratch=(), out_specs=None):
        return pl.pallas_call(
            body,
            out_shape=out_shape,
            in_specs=in_specs,
            out_specs=VMEM if out_specs is None else out_specs,
            scratch_shapes=scratch,
            compiler_params=pltpu.CompilerParams(vmem_limit_bytes=LIMIT),
            cost_estimate=pl.CostEstimate(flops=flops, bytes_accessed=moved, transcendentals=0),
            name=name,
        )

    pieces = jax.ShapeDtypeStruct((2, 2, HALF, WIN), jnp.float32)
    strip = jax.ShapeDtypeStruct(object_slices.shape, jnp.float32)
    window = (pltpu.VMEM((2, WIN, WIN), jnp.float32),)
    tables = jnp.asarray(np.stack(build_tables()))
    other_slice = lax.ppermute(object_slices, "cuts", [(0, 1), (1, 0)])
    pos_second = send(positions, 1, 1, second)
    again, own_slice = kernel(
        stage_kernel,
        "stage",
        (jax.ShapeDtypeStruct(positions.shape, positions.dtype), strip),
        [SMEM, ANY],
        0,
        4 << 20,
        (pltpu.SemaphoreType.DMA,),
        (SMEM, VMEM),
    )(positions, object_slices)
    pos_first = send(again, 1, 1, first)

    def cut(name, place, source, after):
        return kernel(cut_kernel, name, pieces, [SMEM, VMEM, ANY], 0, 1 << 20)(place, source, after)

    to_second_zero = cut("cut_second_zero", pos_second, other_slice, pos_first)
    to_first_zero = cut("cut_first_zero", pos_first, other_slice, to_second_zero)
    to_second_one = cut("cut_second_one", pos_second, own_slice, to_first_zero)
    to_first_one = cut("cut_first_one", pos_first, own_slice, to_second_one)
    second_zero = send(to_second_zero, 1, 0, second)
    first_zero = send(to_first_zero, 1, 0, first)
    second_one = send(to_second_one, 1, 0, second)
    first_one = send(to_first_one, 1, 0, first)
    second_copy = send(pos_second, 1, 0, same)
    first_copy = send(pos_first, 1, 0, same)
    wave = kernel(
        enter_kernel,
        "enter",
        jax.ShapeDtypeStruct((2, 2, 2, WIN, WIN), jnp.float32),
        [SMEM] * 2 + [VMEM] * 5 + [ANY] * 2,
        18 * 2 * WIN**3,
        3 << 20,
        window,
    )(positions, counts, probe, tables, own_slice, second_zero, first_zero, second_copy, first_copy)
    rim_zero, rim_one, mid_zero, mid_one = kernel(
        slot_kernel,
        "slot",
        (pieces,) * 4,
        [SMEM] * 2 + [VMEM] * 6,
        54 * 2 * WIN**3,
        6 << 20,
        window,
        (VMEM,) * 4,
    )(positions, counts, tables, wave, other_slice, second_one, first_one, intensity)
    back_second_zero = send(rim_zero, 0, 1, second)
    back_first_zero = send(rim_zero, 0, 1, first)
    back_second_one = send(rim_one, 0, 1, second)
    back_first_one = send(rim_one, 0, 1, first)
    mid_one = send(mid_one, 0, 1, same)
    return kernel(collect_kernel, "collect", strip, [SMEM] * 5 + [VMEM] * 6, 0, 4 << 20)(
        positions,
        pos_second,
        pos_first,
        second_copy,
        first_copy,
        mid_zero,
        send(back_second_zero, 1, 0, same),
        send(back_first_zero, 1, 0, same),
        back_second_one,
        back_first_one,
        mid_one,
    )


def solution(mesh):
    in_specs = (
        P("cuts", None, "tile", None),
        P(),
        P("tile", None),
        P("tile"),
        P("tile", None, None),
    )
    out_specs = P("cuts", None, "tile", None)
    return jax.shard_map(local, mesh=mesh, in_specs=in_specs, out_specs=out_specs, check_vma=False)
```

```python
import numpy as np
import ml_dtypes

import jax
import jax.numpy as jnp
from jax import lax
from jax.experimental import pallas as pl
from jax.experimental.pallas import tpu as pltpu
from jax.sharding import PartitionSpec as P

WIN = 256
HALF = 128


def split_tables(real_part, imag_part):
    parts = []
    for values in (real_part, imag_part - real_part, real_part + imag_part):
        high = values.astype(ml_dtypes.bfloat16)
        low = (values - high.astype(np.float64)).astype(ml_dtypes.bfloat16)
        parts += [high, low]
    return np.stack(parts)


def build_tables():
    index = np.arange(WIN)
    turned = 2.0 * np.pi * ((index[:, None] * index[None, :]) % WIN) / WIN
    dft = (np.cos(turned) - 1j * np.sin(turned)) / np.sqrt(WIN)
    centred = (index + WIN // 2) % WIN - WIN // 2
    phase = np.pi * (centred * centred % (4 * WIN)) / (2 * WIN)
    prop = np.conj(dft) @ ((np.cos(phase) - 1j * np.sin(phase))[:, None] * dft)
    prop = 0.5 * (prop + prop.T)
    return split_tables(dft.real, dft.imag), split_tables(prop.real, prop.imag)


def split(value):
    high = value.astype(jnp.bfloat16)
    low = (value - high.astype(jnp.float32)).astype(jnp.bfloat16)
    return high, low


def dot(left, right):
    return jnp.dot(left, right, preferred_element_type=jnp.float32)


def product(field, table, which, from_left):
    high, low = split(field)
    table_high = table[2 * which]
    table_low = table[2 * which + 1]
    if from_left:
        return dot(table_high, high) + (dot(table_high, low) + dot(table_low, high))
    return dot(high, table_high) + (dot(low, table_high) + dot(high, table_low))


def complex_product(real, imag, table, conjugate, from_left):
    shared = product(real + imag, table, 0, from_left)
    if conjugate:
        first = product(real, table, 2, from_left)
        second = product(imag, table, 1, from_left)
        return shared + second, shared - first
    first = product(real, table, 1, from_left)
    second = product(imag, table, 2, from_left)
    return shared - second, shared + first


def sandwich(real, imag, table, conjugate):
    real, imag = complex_product(real, imag, table, conjugate, False)
    return complex_product(real, imag, table, conjugate, True)


def block(number):
    return pl.ds(pl.multiple_of(number * HALF, HALF), HALF)


def cut_piece(strip_ref, column, out_ref):
    first = lax.shift_right_logical(column, 7)
    offset = jnp.bitwise_and(column, HALF - 1)
    lanes = lax.broadcasted_iota(jnp.int32, (HALF, HALF), 1)
    mine = lanes >= offset
    third = jnp.minimum(first + 2, strip_ref.shape[-1] // HALF - 1)
    for part in range(2):
        out_ref[part, :, 0:HALF] = jnp.where(
            mine, strip_ref[0, part, :, block(first)], strip_ref[0, part, :, block(third)]
        )
        out_ref[part, :, HALF:WIN] = strip_ref[0, part, :, block(first + 1)]


def stage_kernel(strip_ref, out_ref, sem):
    copy = pltpu.make_async_copy(strip_ref, out_ref, sem)
    copy.start()
    copy.wait()


def cut_kernel(first_ref, second_ref, strip_ref, to_first_ref, to_second_ref):
    @pl.when(lax.axis_index("cuts") == 1)
    def _():
        for slot in range(2):
            cut_piece(strip_ref, first_ref[slot, 1], to_first_ref.at[slot])
        for slot in range(2):
            cut_piece(strip_ref, second_ref[slot, 1], to_second_ref.at[slot])


def slots_of_core(counts_ref):
    return jnp.where(lax.axis_index("cuts") == 0, counts_ref[0], 0)


def fill_window(pos_ref, slot, strip_ref, first_ref, second_ref, window_ref):
    tile = lax.axis_index("tile")
    odd = jnp.bitwise_and(tile, 1)
    shift_rows = pos_ref[slot, 0] - (tile - 1) * HALF
    column = pos_ref[slot, 1]
    rows = lax.broadcasted_iota(jnp.int32, (HALF, WIN), 0)
    from_first = (1 - 2 * odd) * (rows - shift_rows) >= odd
    for part in range(2):
        window_ref[part, 0:HALF] = jnp.where(
            from_first, first_ref[slot, part], second_ref[slot, part]
        )
    cut_piece(strip_ref, column, window_ref.at[:, HALF:WIN])
    return shift_rows, jnp.bitwise_and(column, HALF - 1)


def enter_kernel(
    pos_ref,
    counts_ref,
    probe_ref,
    table_ref,
    own_ref,
    first_ref,
    second_ref,
    first_copy_ref,
    second_copy_ref,
    wave_ref,
    window_ref,
):
    @pl.loop(0, slots_of_core(counts_ref))
    def _(slot):
        shift_rows, shift_cols = fill_window(pos_ref, slot, own_ref, first_ref, second_ref, window_ref)

        def rolled(part):
            return pltpu.roll(pltpu.roll(probe_ref[part], shift_rows, 0), shift_cols, 1)

        zero_re, zero_im = rolled(0), rolled(1)
        wave_ref[slot, 0, 0] = zero_re
        wave_ref[slot, 0, 1] = zero_im
        cell_re, cell_im = window_ref[0], window_ref[1]
        one_re, one_im = sandwich(
            zero_re * cell_re - zero_im * cell_im,
            zero_re * cell_im + zero_im * cell_re,
            table_ref.at[1],
            False,
        )
        wave_ref[slot, 1, 0] = one_re
        wave_ref[slot, 1, 1] = one_im


def slot_kernel(
    pos_ref,
    counts_ref,
    table_ref,
    wave_ref,
    other_ref,
    first_ref,
    second_ref,
    intensity_ref,
    rim_zero_ref,
    rim_one_ref,
    mid_zero_ref,
    mid_one_ref,
    window_ref,
):
    live_slots = slots_of_core(counts_ref)
    dft_ref, prop_ref = table_ref.at[0], table_ref.at[1]

    @pl.loop(0, live_slots)
    def _(slot):
        fill_window(pos_ref, slot, other_ref, first_ref, second_ref, window_ref)
        cell_re, cell_im = window_ref[0], window_ref[1]
        one_re, one_im = wave_ref[slot, 1, 0], wave_ref[slot, 1, 1]
        far_re, far_im = sandwich(
            one_re * cell_re - one_im * cell_im,
            one_re * cell_im + one_im * cell_re,
            dft_ref,
            False,
        )
        residual = far_re * far_re + far_im * far_im - intensity_ref[slot]
        back_re, back_im = sandwich(far_re * residual, far_im * residual, dft_ref, True)
        for part, value in (
            (0, one_re * back_re + one_im * back_im),
            (1, one_re * back_im - one_im * back_re),
        ):
            rim_one_ref[slot, part] = value[0:HALF]
            mid_one_ref[slot, part] = value[HALF:WIN]
        back_re, back_im = sandwich(
            cell_re * back_re + cell_im * back_im,
            cell_re * back_im - cell_im * back_re,
            prop_ref,
            True,
        )
        zero_re, zero_im = wave_ref[slot, 0, 0], wave_ref[slot, 0, 1]
        for part, value in (
            (0, zero_re * back_re + zero_im * back_im),
            (1, zero_re * back_im - zero_im * back_re),
        ):
            rim_zero_ref[slot, part] = value[0:HALF]
            mid_zero_ref[slot, part] = value[HALF:WIN]

    @pl.when(live_slots == 1)
    def _():
        for ref in (rim_zero_ref, rim_one_ref, mid_zero_ref, mid_one_ref):
            ref[1] = jnp.zeros_like(ref[1])


def add_piece(out_ref, piece_ref, column, keep):
    first = lax.shift_right_logical(column, 7)
    offset = jnp.bitwise_and(column, HALF - 1)
    lanes = lax.broadcasted_iota(jnp.int32, (HALF, HALF), 1)
    mine = lanes >= offset
    third = jnp.minimum(first + 2, out_ref.shape[-1] // HALF - 1)
    for part in range(2):
        left = piece_ref[part, :, 0:HALF]
        right = piece_ref[part, :, HALF:WIN]
        if keep is not None:
            left = jnp.where(keep, left, 0.0)
            right = jnp.where(keep, right, 0.0)
        out_ref[0, part, :, block(first)] += jnp.where(mine, left, 0.0)
        out_ref[0, part, :, block(first + 1)] += right
        out_ref[0, part, :, block(third)] += jnp.where(mine, 0.0, left)


def collect_kernel(
    pos_ref,
    first_ref,
    second_ref,
    first_copy_ref,
    second_copy_ref,
    mid_zero_ref,
    first_zero_ref,
    second_zero_ref,
    first_one_ref,
    second_one_ref,
    mid_one_ref,
    out_ref,
):
    core = lax.axis_index("cuts")
    tile = lax.axis_index("tile")
    odd = jnp.bitwise_and(tile, 1)
    out_ref[...] = jnp.zeros_like(out_ref)
    rows = lax.broadcasted_iota(jnp.int32, (HALF, HALF), 0)

    def gather(mid_ref, *nearby):
        for slot in range(2):
            add_piece(out_ref, mid_ref.at[slot], pos_ref[slot, 1], None)
        for piece_ref, place_ref, above in nearby:
            sign = 2 * above - 1
            for slot in range(2):
                shift_rows = place_ref[slot, 0] - (tile + sign - 1) * HALF
                keep = sign * (rows - shift_rows) >= 1 - above
                add_piece(out_ref, piece_ref.at[slot], place_ref[slot, 1], keep)

    @pl.when(core == 0)
    def _():
        gather(
            mid_zero_ref,
            (first_zero_ref, first_copy_ref, odd),
            (second_zero_ref, second_copy_ref, 1 - odd),
        )

    @pl.when(core == 1)
    def _():
        gather(
            mid_one_ref,
            (first_one_ref, first_ref, odd),
            (second_one_ref, second_ref, 1 - odd),
        )


SMEM = pl.BlockSpec(memory_space=pltpu.SMEM)
VMEM = pl.BlockSpec(memory_space=pltpu.VMEM)
ANY = pl.BlockSpec(memory_space=pl.ANY)


LIMIT = 12 << 20


def local(object_slices, probe, positions, counts, intensity):
    tiles = lax.axis_size("tile")

    def first(tile):
        return ((tile + 1) ^ 1) - 1

    def second(tile):
        return tile ^ 1

    def same(tile):
        return tile

    def send(value, source, target, partner):
        pairs = [(tile, partner(tile)) for tile in range(tiles) if 0 <= partner(tile) < tiles]
        pairs = [(source * tiles + one, target * tiles + two) for one, two in pairs]
        return lax.ppermute(value, ("cuts", "tile"), pairs)

    def kernel(body, name, out_shape, in_specs, flops, moved, scratch=(), out_specs=None):
        return pl.pallas_call(
            body,
            out_shape=out_shape,
            in_specs=in_specs,
            out_specs=VMEM if out_specs is None else out_specs,
            scratch_shapes=scratch,
            compiler_params=pltpu.CompilerParams(vmem_limit_bytes=LIMIT),
            cost_estimate=pl.CostEstimate(flops=flops, bytes_accessed=moved, transcendentals=0),
            name=name,
        )

    pieces = jax.ShapeDtypeStruct((2, 2, HALF, WIN), jnp.float32)
    strip = jax.ShapeDtypeStruct(object_slices.shape, jnp.float32)
    window = (pltpu.VMEM((2, WIN, WIN), jnp.float32),)
    tables = jnp.asarray(np.stack(build_tables()))
    other_slice = lax.ppermute(object_slices, "cuts", [(0, 1), (1, 0)])
    pos_first = send(positions, 1, 1, first)
    pos_second = send(positions, 1, 1, second)
    own_slice = kernel(
        stage_kernel, "stage", strip, [ANY], 0, 4 << 20, (pltpu.SemaphoreType.DMA,)
    )(object_slices)

    def cut(name, source):
        return kernel(
            cut_kernel, name, (pieces,) * 2, [SMEM] * 2 + [VMEM], 0, 2 << 20, (), (VMEM,) * 2
        )(pos_first, pos_second, source)

    to_first_zero, to_second_zero = cut("cut_zero", other_slice)
    second_zero = send(to_second_zero, 1, 0, second)
    first_zero = send(to_first_zero, 1, 0, first)
    to_first_one, to_second_one = cut("cut_one", own_slice)
    second_one = send(to_second_one, 1, 0, second)
    first_one = send(to_first_one, 1, 0, first)
    second_copy = send(pos_second, 1, 0, same)
    first_copy = send(pos_first, 1, 0, same)
    wave = kernel(
        enter_kernel,
        "enter",
        jax.ShapeDtypeStruct((2, 2, 2, WIN, WIN), jnp.float32),
        [SMEM] * 2 + [VMEM] * 5 + [ANY] * 2,
        18 * 2 * WIN**3,
        3 << 20,
        window,
    )(positions, counts, probe, tables, own_slice, first_zero, second_zero, first_copy, second_copy)
    rim_zero, rim_one, mid_zero, mid_one = kernel(
        slot_kernel,
        "slot",
        (pieces,) * 4,
        [SMEM] * 2 + [VMEM] * 6,
        54 * 2 * WIN**3,
        6 << 20,
        window,
        (VMEM,) * 4,
    )(positions, counts, tables, wave, other_slice, first_one, second_one, intensity)
    back_first_zero = send(rim_zero, 0, 1, first)
    back_second_zero = send(rim_zero, 0, 1, second)
    back_first_one = send(rim_one, 0, 1, first)
    back_second_one = send(rim_one, 0, 1, second)
    mid_one = send(mid_one, 0, 1, same)
    return kernel(collect_kernel, "collect", strip, [SMEM] * 5 + [VMEM] * 6, 0, 4 << 20)(
        positions,
        pos_first,
        pos_second,
        first_copy,
        second_copy,
        mid_zero,
        send(back_first_zero, 1, 0, same),
        send(back_second_zero, 1, 0, same),
        back_first_one,
        back_second_one,
        mid_one,
    )


def solution(mesh):
    in_specs = (
        P("cuts", None, "tile", None),
        P(),
        P("tile", None),
        P("tile"),
        P("tile", None, None),
    )
    out_specs = P("cuts", None, "tile", None)
    return jax.shard_map(local, mesh=mesh, in_specs=in_specs, out_specs=out_specs, check_vma=False)
```

```python
import numpy as np
import ml_dtypes

import jax
import jax.numpy as jnp
from jax import lax
from jax.experimental import pallas as pl
from jax.experimental.pallas import tpu as pltpu
from jax.sharding import PartitionSpec as P

WIN = 256
HALF = 128
CHUNK = 64


def split_tables(real_part, imag_part):
    parts = []
    for values in (real_part, imag_part - real_part, real_part + imag_part):
        high = values.astype(ml_dtypes.bfloat16)
        low = (values - high.astype(np.float64)).astype(ml_dtypes.bfloat16)
        parts += [high, low]
    return np.stack(parts)


def build_tables():
    index = np.arange(WIN)
    turned = 2.0 * np.pi * ((index[:, None] * index[None, :]) % WIN) / WIN
    dft = (np.cos(turned) - 1j * np.sin(turned)) / np.sqrt(WIN)
    centred = (index + WIN // 2) % WIN - WIN // 2
    phase = np.pi * (centred * centred % (4 * WIN)) / (2 * WIN)
    prop = np.conj(dft) @ ((np.cos(phase) - 1j * np.sin(phase))[:, None] * dft)
    prop = 0.5 * (prop + prop.T)
    return split_tables(dft.real, dft.imag), split_tables(prop.real, prop.imag)


def split(value):
    high = value.astype(jnp.bfloat16)
    low = (value - high.astype(jnp.float32)).astype(jnp.bfloat16)
    return high, low


def dot(left, right):
    return jnp.dot(left, right, preferred_element_type=jnp.float32)


def product(field, table, which, from_left):
    high, low = split(field)
    table_high = table[2 * which]
    tables = [table_high, table_high, table[2 * which + 1]]
    if from_left:
        return dot(jnp.concatenate(tables, axis=1), jnp.concatenate([high, low, high], axis=0))
    return dot(jnp.concatenate([high, low, high], axis=1), jnp.concatenate(tables, axis=0))


def complex_product(real, imag, table, conjugate, from_left):
    shared = product(real + imag, table, 0, from_left)
    if conjugate:
        first = product(real, table, 2, from_left)
        second = product(imag, table, 1, from_left)
        return shared + second, shared - first
    first = product(real, table, 1, from_left)
    second = product(imag, table, 2, from_left)
    return shared - second, shared + first


def sandwich(real, imag, table, conjugate):
    real, imag = complex_product(real, imag, table, conjugate, False)
    return complex_product(real, imag, table, conjugate, True)


def block(number):
    return pl.ds(pl.multiple_of(number * HALF, HALF), HALF)


def cut_piece(strip_ref, column, out_ref):
    first = lax.shift_right_logical(column, 7)
    offset = jnp.bitwise_and(column, HALF - 1)
    lanes = lax.broadcasted_iota(jnp.int32, (HALF, HALF), 1)
    mine = lanes >= offset
    third = jnp.minimum(first + 2, strip_ref.shape[-1] // HALF - 1)
    for part in range(2):
        out_ref[part, :, 0:HALF] = jnp.where(
            mine, strip_ref[0, part, :, block(first)], strip_ref[0, part, :, block(third)]
        )
        out_ref[part, :, HALF:WIN] = strip_ref[0, part, :, block(first + 1)]


def stage_kernel(strip_ref, out_ref, sem):
    copy = pltpu.make_async_copy(strip_ref, out_ref, sem)
    copy.start()
    copy.wait()


def cut_kernel(first_ref, second_ref, strip_ref, to_first_ref, to_second_ref):
    @pl.when(lax.axis_index("cuts") == 1)
    def _():
        for slot in range(2):
            cut_piece(strip_ref, first_ref[slot, 1], to_first_ref.at[slot])
        for slot in range(2):
            cut_piece(strip_ref, second_ref[slot, 1], to_second_ref.at[slot])


def slots_of_core(counts_ref):
    return jnp.where(lax.axis_index("cuts") == 0, counts_ref[0], 0)


def fill_window(pos_ref, slot, strip_ref, first_ref, second_ref, window_ref):
    tile = lax.axis_index("tile")
    odd = jnp.bitwise_and(tile, 1)
    shift_rows = pos_ref[slot, 0] - (tile - 1) * HALF
    column = pos_ref[slot, 1]
    rows = lax.broadcasted_iota(jnp.int32, (HALF, WIN), 0)
    from_first = (1 - 2 * odd) * (rows - shift_rows) >= odd
    for part in range(2):
        window_ref[part, 0:HALF] = jnp.where(
            from_first, first_ref[slot, part], second_ref[slot, part]
        )
    cut_piece(strip_ref, column, window_ref.at[:, HALF:WIN])
    return shift_rows, jnp.bitwise_and(column, HALF - 1)


def enter_kernel(
    pos_ref,
    counts_ref,
    probe_ref,
    table_ref,
    own_ref,
    first_ref,
    second_ref,
    first_copy_ref,
    second_copy_ref,
    wave_ref,
    window_ref,
):
    @pl.loop(0, slots_of_core(counts_ref))
    def _(slot):
        shift_rows, shift_cols = fill_window(pos_ref, slot, own_ref, first_ref, second_ref, window_ref)

        def rolled(part):
            return pltpu.roll(pltpu.roll(probe_ref[part], shift_rows, 0), shift_cols, 1)

        zero_re, zero_im = rolled(0), rolled(1)
        wave_ref[slot, 0, 0] = zero_re
        wave_ref[slot, 0, 1] = zero_im
        cell_re, cell_im = window_ref[0], window_ref[1]
        one_re, one_im = sandwich(
            zero_re * cell_re - zero_im * cell_im,
            zero_re * cell_im + zero_im * cell_re,
            table_ref.at[1],
            False,
        )
        wave_ref[slot, 1, 0] = one_re
        wave_ref[slot, 1, 1] = one_im


def slot_kernel(
    pos_ref,
    counts_ref,
    table_ref,
    wave_ref,
    other_ref,
    first_ref,
    second_ref,
    intensity_ref,
    rim_zero_ref,
    rim_one_ref,
    mid_zero_ref,
    mid_one_ref,
    window_ref,
):
    live_slots = slots_of_core(counts_ref)
    dft_ref, prop_ref = table_ref.at[0], table_ref.at[1]

    @pl.loop(0, live_slots)
    def _(slot):
        fill_window(pos_ref, slot, other_ref, first_ref, second_ref, window_ref)
        cell_re, cell_im = window_ref[0], window_ref[1]
        one_re, one_im = wave_ref[slot, 1, 0], wave_ref[slot, 1, 1]
        far_re, far_im = sandwich(
            one_re * cell_re - one_im * cell_im,
            one_re * cell_im + one_im * cell_re,
            dft_ref,
            False,
        )
        residual = far_re * far_re + far_im * far_im - intensity_ref[slot]
        back_re, back_im = sandwich(far_re * residual, far_im * residual, dft_ref, True)
        for part, value in (
            (0, one_re * back_re + one_im * back_im),
            (1, one_re * back_im - one_im * back_re),
        ):
            rim_one_ref[slot, part] = value[0:HALF]
            mid_one_ref[slot, part] = value[HALF:WIN]
        back_re, back_im = sandwich(
            cell_re * back_re + cell_im * back_im,
            cell_re * back_im - cell_im * back_re,
            prop_ref,
            True,
        )
        zero_re, zero_im = wave_ref[slot, 0, 0], wave_ref[slot, 0, 1]
        for part, value in (
            (0, zero_re * back_re + zero_im * back_im),
            (1, zero_re * back_im - zero_im * back_re),
        ):
            rim_zero_ref[slot, part] = value[0:HALF]
            mid_zero_ref[slot, part] = value[HALF:WIN]

    @pl.when(live_slots == 1)
    def _():
        for ref in (rim_zero_ref, rim_one_ref, mid_zero_ref, mid_one_ref):
            ref[1] = jnp.zeros_like(ref[1])


def add_piece(out_ref, piece_ref, column, keep):
    first = lax.shift_right_logical(column, 7)
    offset = jnp.bitwise_and(column, HALF - 1)
    mine = lax.broadcasted_iota(jnp.int32, (CHUNK, HALF), 1) >= offset
    third = jnp.minimum(first + 2, out_ref.shape[-1] // HALF - 1)
    left = piece_ref[:, 0:HALF]
    right = piece_ref[:, HALF:WIN]
    if keep is not None:
        left = jnp.where(keep, left, 0.0)
        right = jnp.where(keep, right, 0.0)
    out_ref[:, block(first)] += jnp.where(mine, left, 0.0)
    out_ref[:, block(first + 1)] += right
    out_ref[:, block(third)] += jnp.where(mine, 0.0, left)


def collect_kernel(
    pos_ref,
    first_ref,
    second_ref,
    first_copy_ref,
    second_copy_ref,
    mid_zero_ref,
    first_zero_ref,
    second_zero_ref,
    first_one_ref,
    second_one_ref,
    mid_one_ref,
    out_ref,
    sum_ref,
    sem,
):
    core = lax.axis_index("cuts")
    tile = lax.axis_index("tile")
    odd = jnp.bitwise_and(tile, 1)
    rows = lax.broadcasted_iota(jnp.int32, (CHUNK, HALF), 0)

    def gather(mid_ref, *nearby):
        copies = []
        for part in range(2):
            for top in range(0, HALF, CHUNK):
                here = pl.ds(top, CHUNK)
                total = sum_ref.at[part, here]
                total[...] = jnp.zeros(total.shape, jnp.float32)
                for slot in range(2):
                    add_piece(total, mid_ref.at[slot, part, here], pos_ref[slot, 1], None)
                for piece_ref, place_ref, above in nearby:
                    sign = 2 * above - 1
                    for slot in range(2):
                        shift_rows = place_ref[slot, 0] - (tile + sign - 1) * HALF - top
                        keep = sign * (rows - shift_rows) >= 1 - above
                        piece = piece_ref.at[slot, part, here]
                        add_piece(total, piece, place_ref[slot, 1], keep)
                copy = pltpu.make_async_copy(
                    total, out_ref.at[0, part, here], sem.at[len(copies)]
                )
                copy.start()
                copies.append(copy)
        for copy in copies:
            copy.wait()

    @pl.when(core == 0)
    def _():
        gather(
            mid_zero_ref,
            (first_zero_ref, first_copy_ref, odd),
            (second_zero_ref, second_copy_ref, 1 - odd),
        )

    @pl.when(core == 1)
    def _():
        gather(
            mid_one_ref,
            (first_one_ref, first_ref, odd),
            (second_one_ref, second_ref, 1 - odd),
        )


SMEM = pl.BlockSpec(memory_space=pltpu.SMEM)
VMEM = pl.BlockSpec(memory_space=pltpu.VMEM)
ANY = pl.BlockSpec(memory_space=pl.ANY)


LIMIT = 12 << 20


def local(object_slices, probe, positions, counts, intensity):
    tiles = lax.axis_size("tile")

    def first(tile):
        return ((tile + 1) ^ 1) - 1

    def second(tile):
        return tile ^ 1

    def same(tile):
        return tile

    def send(value, source, target, partner):
        pairs = [(tile, partner(tile)) for tile in range(tiles) if 0 <= partner(tile) < tiles]
        pairs = [(source * tiles + one, target * tiles + two) for one, two in pairs]
        return lax.ppermute(value, ("cuts", "tile"), pairs)

    def kernel(body, name, out_shape, in_specs, flops, moved, scratch=(), out_specs=None):
        return pl.pallas_call(
            body,
            out_shape=out_shape,
            in_specs=in_specs,
            out_specs=VMEM if out_specs is None else out_specs,
            scratch_shapes=scratch,
            compiler_params=pltpu.CompilerParams(vmem_limit_bytes=LIMIT),
            cost_estimate=pl.CostEstimate(flops=flops, bytes_accessed=moved, transcendentals=0),
            name=name,
        )

    pieces = jax.ShapeDtypeStruct((2, 2, HALF, WIN), jnp.float32)
    strip = jax.ShapeDtypeStruct(object_slices.shape, jnp.float32)
    window = (pltpu.VMEM((2, WIN, WIN), jnp.float32),)
    tables = jnp.asarray(np.stack(build_tables()))
    other_slice = lax.ppermute(object_slices, "cuts", [(0, 1), (1, 0)])
    pos_first = send(positions, 1, 1, first)
    pos_second = send(positions, 1, 1, second)
    own_slice = kernel(
        stage_kernel, "stage", strip, [ANY], 0, 4 << 20, (pltpu.SemaphoreType.DMA,)
    )(object_slices)

    def cut(name, source):
        return kernel(
            cut_kernel, name, (pieces,) * 2, [SMEM] * 2 + [VMEM], 0, 2 << 20, (), (VMEM,) * 2
        )(pos_first, pos_second, source)

    to_first_zero, to_second_zero = cut("cut_zero", other_slice)
    second_zero = send(to_second_zero, 1, 0, second)
    first_zero = send(to_first_zero, 1, 0, first)
    to_first_one, to_second_one = cut("cut_one", own_slice)
    second_one = send(to_second_one, 1, 0, second)
    first_one = send(to_first_one, 1, 0, first)
    second_copy = send(pos_second, 1, 0, same)
    first_copy = send(pos_first, 1, 0, same)
    wave = kernel(
        enter_kernel,
        "enter",
        jax.ShapeDtypeStruct((2, 2, 2, WIN, WIN), jnp.float32),
        [SMEM] * 2 + [VMEM] * 5 + [ANY] * 2,
        18 * 2 * WIN**3,
        3 << 20,
        window,
    )(positions, counts, probe, tables, own_slice, first_zero, second_zero, first_copy, second_copy)
    rim_zero, rim_one, mid_zero, mid_one = kernel(
        slot_kernel,
        "slot",
        (pieces,) * 4,
        [SMEM] * 2 + [VMEM] * 6,
        54 * 2 * WIN**3,
        6 << 20,
        window,
        (VMEM,) * 4,
    )(positions, counts, tables, wave, other_slice, first_one, second_one, intensity)
    back_first_zero = send(rim_zero, 0, 1, first)
    back_second_zero = send(rim_zero, 0, 1, second)
    back_first_one = send(rim_one, 0, 1, first)
    back_second_one = send(rim_one, 0, 1, second)
    mid_one = send(mid_one, 0, 1, same)
    return kernel(
        collect_kernel,
        "collect",
        strip,
        [SMEM] * 5 + [VMEM] * 6,
        0,
        4 << 20,
        (pltpu.VMEM(strip.shape[1:], jnp.float32), pltpu.SemaphoreType.DMA((2 * HALF // CHUNK,))),
        ANY,
    )(
        positions,
        pos_first,
        pos_second,
        first_copy,
        second_copy,
        mid_zero,
        send(back_first_zero, 1, 0, same),
        send(back_second_zero, 1, 0, same),
        back_first_one,
        back_second_one,
        mid_one,
    )


def solution(mesh):
    in_specs = (
        P("cuts", None, "tile", None),
        P(),
        P("tile", None),
        P("tile"),
        P("tile", None, None),
    )
    out_specs = P("cuts", None, "tile", None)
    return jax.shard_map(local, mesh=mesh, in_specs=in_specs, out_specs=out_specs, check_vma=False)
```

```python
import numpy as np
import ml_dtypes

import jax
import jax.numpy as jnp
from jax import lax
from jax.experimental import pallas as pl
from jax.experimental.pallas import tpu as pltpu
from jax.sharding import PartitionSpec as P

WIN = 256
HALF = 128
CHUNK = 64


def split_tables(real_part, imag_part):
    parts = []
    for values in (real_part, imag_part, -imag_part):
        high = values.astype(ml_dtypes.bfloat16)
        low = (values - high.astype(np.float64)).astype(ml_dtypes.bfloat16)
        parts += [high, low]
    return np.stack(parts)


def build_tables():
    index = np.arange(WIN)
    turned = 2.0 * np.pi * ((index[:, None] * index[None, :]) % WIN) / WIN
    dft = (np.cos(turned) - 1j * np.sin(turned)) / np.sqrt(WIN)
    centred = (index + WIN // 2) % WIN - WIN // 2
    phase = np.pi * (centred * centred % (4 * WIN)) / (2 * WIN)
    prop = np.conj(dft) @ ((np.cos(phase) - 1j * np.sin(phase))[:, None] * dft)
    prop = 0.5 * (prop + prop.T)
    return split_tables(dft.real, dft.imag), split_tables(prop.real, prop.imag)


def split(value):
    high = value.astype(jnp.bfloat16)
    low = (value - high.astype(jnp.float32)).astype(jnp.bfloat16)
    return high, low


def dot(left, right):
    return jnp.dot(left, right, preferred_element_type=jnp.float32)


def complex_product(real, imag, table, conjugate, from_left):
    real_high, real_low = split(real)
    imag_high, imag_low = split(imag)
    fields = [real_high, real_low, real_high, imag_high, imag_low, imag_high]

    def terms(which):
        return [table[2 * which], table[2 * which], table[2 * which + 1]]

    plus, minus = (2, 1) if conjugate else (1, 2)
    results = []
    for parts in (terms(0) + terms(minus), terms(plus) + terms(0)):
        if from_left:
            left, right = jnp.concatenate(parts, axis=1), jnp.concatenate(fields, axis=0)
        else:
            left, right = jnp.concatenate(fields, axis=1), jnp.concatenate(parts, axis=0)
        results.append(dot(left, right))
    return results


def sandwich(real, imag, table, conjugate):
    real, imag = complex_product(real, imag, table, conjugate, False)
    return complex_product(real, imag, table, conjugate, True)


def block(number):
    return pl.ds(pl.multiple_of(number * HALF, HALF), HALF)


def cut_piece(strip_ref, column, out_ref):
    first = lax.shift_right_logical(column, 7)
    offset = jnp.bitwise_and(column, HALF - 1)
    lanes = lax.broadcasted_iota(jnp.int32, (HALF, HALF), 1)
    mine = lanes >= offset
    third = jnp.minimum(first + 2, strip_ref.shape[-1] // HALF - 1)
    for part in range(2):
        out_ref[part, :, 0:HALF] = jnp.where(
            mine, strip_ref[0, part, :, block(first)], strip_ref[0, part, :, block(third)]
        )
        out_ref[part, :, HALF:WIN] = strip_ref[0, part, :, block(first + 1)]


def stage_kernel(strip_ref, out_ref, sem):
    copy = pltpu.make_async_copy(strip_ref, out_ref, sem)
    copy.start()
    copy.wait()


def cut_kernel(first_ref, second_ref, strip_ref, to_first_ref, to_second_ref):
    @pl.when(lax.axis_index("cuts") == 1)
    def _():
        for slot in range(2):
            cut_piece(strip_ref, first_ref[slot, 1], to_first_ref.at[slot])
        for slot in range(2):
            cut_piece(strip_ref, second_ref[slot, 1], to_second_ref.at[slot])


def slots_of_core(counts_ref):
    return jnp.where(lax.axis_index("cuts") == 0, counts_ref[0], 0)


def fill_window(pos_ref, slot, strip_ref, first_ref, second_ref, window_ref):
    tile = lax.axis_index("tile")
    odd = jnp.bitwise_and(tile, 1)
    shift_rows = pos_ref[slot, 0] - (tile - 1) * HALF
    column = pos_ref[slot, 1]
    rows = lax.broadcasted_iota(jnp.int32, (HALF, WIN), 0)
    from_first = (1 - 2 * odd) * (rows - shift_rows) >= odd
    for part in range(2):
        window_ref[part, 0:HALF] = jnp.where(
            from_first, first_ref[slot, part], second_ref[slot, part]
        )
    cut_piece(strip_ref, column, window_ref.at[:, HALF:WIN])
    return shift_rows, jnp.bitwise_and(column, HALF - 1)


def enter_kernel(
    pos_ref,
    counts_ref,
    probe_ref,
    table_ref,
    own_ref,
    first_ref,
    second_ref,
    first_copy_ref,
    second_copy_ref,
    wave_ref,
    window_ref,
):
    @pl.loop(0, slots_of_core(counts_ref))
    def _(slot):
        shift_rows, shift_cols = fill_window(pos_ref, slot, own_ref, first_ref, second_ref, window_ref)

        def rolled(part):
            return pltpu.roll(pltpu.roll(probe_ref[part], shift_rows, 0), shift_cols, 1)

        zero_re, zero_im = rolled(0), rolled(1)
        wave_ref[slot, 0, 0] = zero_re
        wave_ref[slot, 0, 1] = zero_im
        cell_re, cell_im = window_ref[0], window_ref[1]
        one_re, one_im = sandwich(
            zero_re * cell_re - zero_im * cell_im,
            zero_re * cell_im + zero_im * cell_re,
            table_ref.at[1],
            False,
        )
        wave_ref[slot, 1, 0] = one_re
        wave_ref[slot, 1, 1] = one_im


def slot_kernel(
    pos_ref,
    counts_ref,
    table_ref,
    wave_ref,
    other_ref,
    first_ref,
    second_ref,
    intensity_ref,
    rim_zero_ref,
    rim_one_ref,
    mid_zero_ref,
    mid_one_ref,
    window_ref,
):
    live_slots = slots_of_core(counts_ref)
    dft_ref, prop_ref = table_ref.at[0], table_ref.at[1]

    @pl.loop(0, live_slots)
    def _(slot):
        fill_window(pos_ref, slot, other_ref, first_ref, second_ref, window_ref)
        cell_re, cell_im = window_ref[0], window_ref[1]
        one_re, one_im = wave_ref[slot, 1, 0], wave_ref[slot, 1, 1]
        far_re, far_im = sandwich(
            one_re * cell_re - one_im * cell_im,
            one_re * cell_im + one_im * cell_re,
            dft_ref,
            False,
        )
        residual = far_re * far_re + far_im * far_im - intensity_ref[slot]
        back_re, back_im = sandwich(far_re * residual, far_im * residual, dft_ref, True)
        for part, value in (
            (0, one_re * back_re + one_im * back_im),
            (1, one_re * back_im - one_im * back_re),
        ):
            rim_one_ref[slot, part] = value[0:HALF]
            mid_one_ref[slot, part] = value[HALF:WIN]
        back_re, back_im = sandwich(
            cell_re * back_re + cell_im * back_im,
            cell_re * back_im - cell_im * back_re,
            prop_ref,
            True,
        )
        zero_re, zero_im = wave_ref[slot, 0, 0], wave_ref[slot, 0, 1]
        for part, value in (
            (0, zero_re * back_re + zero_im * back_im),
            (1, zero_re * back_im - zero_im * back_re),
        ):
            rim_zero_ref[slot, part] = value[0:HALF]
            mid_zero_ref[slot, part] = value[HALF:WIN]

    @pl.when(live_slots == 1)
    def _():
        for ref in (rim_zero_ref, rim_one_ref, mid_zero_ref, mid_one_ref):
            ref[1] = jnp.zeros_like(ref[1])


def add_piece(out_ref, piece_ref, column, keep):
    first = lax.shift_right_logical(column, 7)
    offset = jnp.bitwise_and(column, HALF - 1)
    mine = lax.broadcasted_iota(jnp.int32, (CHUNK, HALF), 1) >= offset
    third = jnp.minimum(first + 2, out_ref.shape[-1] // HALF - 1)
    left = piece_ref[:, 0:HALF]
    right = piece_ref[:, HALF:WIN]
    if keep is not None:
        left = jnp.where(keep, left, 0.0)
        right = jnp.where(keep, right, 0.0)
    out_ref[:, block(first)] += jnp.where(mine, left, 0.0)
    out_ref[:, block(first + 1)] += right
    out_ref[:, block(third)] += jnp.where(mine, 0.0, left)


def collect_kernel(
    pos_ref,
    first_ref,
    second_ref,
    first_copy_ref,
    second_copy_ref,
    mid_zero_ref,
    first_zero_ref,
    second_zero_ref,
    first_one_ref,
    second_one_ref,
    mid_one_ref,
    out_ref,
    sum_ref,
    sem,
):
    core = lax.axis_index("cuts")
    tile = lax.axis_index("tile")
    odd = jnp.bitwise_and(tile, 1)
    rows = lax.broadcasted_iota(jnp.int32, (CHUNK, HALF), 0)

    def gather(mid_ref, *nearby):
        copies = []
        for part in range(2):
            for top in range(0, HALF, CHUNK):
                here = pl.ds(top, CHUNK)
                total = sum_ref.at[part, here]
                total[...] = jnp.zeros(total.shape, jnp.float32)
                for slot in range(2):
                    add_piece(total, mid_ref.at[slot, part, here], pos_ref[slot, 1], None)
                for piece_ref, place_ref, above in nearby:
                    sign = 2 * above - 1
                    for slot in range(2):
                        shift_rows = place_ref[slot, 0] - (tile + sign - 1) * HALF - top
                        keep = sign * (rows - shift_rows) >= 1 - above
                        piece = piece_ref.at[slot, part, here]
                        add_piece(total, piece, place_ref[slot, 1], keep)
                copy = pltpu.make_async_copy(
                    total, out_ref.at[0, part, here], sem.at[len(copies)]
                )
                copy.start()
                copies.append(copy)
        for copy in copies:
            copy.wait()

    @pl.when(core == 0)
    def _():
        gather(
            mid_zero_ref,
            (first_zero_ref, first_copy_ref, odd),
            (second_zero_ref, second_copy_ref, 1 - odd),
        )

    @pl.when(core == 1)
    def _():
        gather(
            mid_one_ref,
            (first_one_ref, first_ref, odd),
            (second_one_ref, second_ref, 1 - odd),
        )


SMEM = pl.BlockSpec(memory_space=pltpu.SMEM)
VMEM = pl.BlockSpec(memory_space=pltpu.VMEM)
ANY = pl.BlockSpec(memory_space=pl.ANY)


LIMIT = 12 << 20


def local(object_slices, probe, positions, counts, intensity):
    tiles = lax.axis_size("tile")

    def first(tile):
        return ((tile + 1) ^ 1) - 1

    def second(tile):
        return tile ^ 1

    def same(tile):
        return tile

    def send(value, source, target, partner):
        pairs = [(tile, partner(tile)) for tile in range(tiles) if 0 <= partner(tile) < tiles]
        pairs = [(source * tiles + one, target * tiles + two) for one, two in pairs]
        return lax.ppermute(value, ("cuts", "tile"), pairs)

    def kernel(body, name, out_shape, in_specs, flops, moved, scratch=(), out_specs=None):
        return pl.pallas_call(
            body,
            out_shape=out_shape,
            in_specs=in_specs,
            out_specs=VMEM if out_specs is None else out_specs,
            scratch_shapes=scratch,
            compiler_params=pltpu.CompilerParams(vmem_limit_bytes=LIMIT),
            cost_estimate=pl.CostEstimate(flops=flops, bytes_accessed=moved, transcendentals=0),
            name=name,
        )

    pieces = jax.ShapeDtypeStruct((2, 2, HALF, WIN), jnp.float32)
    strip = jax.ShapeDtypeStruct(object_slices.shape, jnp.float32)
    window = (pltpu.VMEM((2, WIN, WIN), jnp.float32),)
    tables = jnp.asarray(np.stack(build_tables()))
    other_slice = lax.ppermute(object_slices, "cuts", [(0, 1), (1, 0)])
    pos_first = send(positions, 1, 1, first)
    pos_second = send(positions, 1, 1, second)
    own_slice = kernel(
        stage_kernel, "stage", strip, [ANY], 0, 4 << 20, (pltpu.SemaphoreType.DMA,)
    )(object_slices)

    def cut(name, source):
        return kernel(
            cut_kernel, name, (pieces,) * 2, [SMEM] * 2 + [VMEM], 0, 2 << 20, (), (VMEM,) * 2
        )(pos_first, pos_second, source)

    to_first_zero, to_second_zero = cut("cut_zero", other_slice)
    second_zero = send(to_second_zero, 1, 0, second)
    first_zero = send(to_first_zero, 1, 0, first)
    to_first_one, to_second_one = cut("cut_one", own_slice)
    second_one = send(to_second_one, 1, 0, second)
    first_one = send(to_first_one, 1, 0, first)
    second_copy = send(pos_second, 1, 0, same)
    first_copy = send(pos_first, 1, 0, same)
    wave = kernel(
        enter_kernel,
        "enter",
        jax.ShapeDtypeStruct((2, 2, 2, WIN, WIN), jnp.float32),
        [SMEM] * 2 + [VMEM] * 5 + [ANY] * 2,
        18 * 2 * WIN**3,
        3 << 20,
        window,
    )(positions, counts, probe, tables, own_slice, first_zero, second_zero, first_copy, second_copy)
    rim_zero, rim_one, mid_zero, mid_one = kernel(
        slot_kernel,
        "slot",
        (pieces,) * 4,
        [SMEM] * 2 + [VMEM] * 6,
        54 * 2 * WIN**3,
        6 << 20,
        window,
        (VMEM,) * 4,
    )(positions, counts, tables, wave, other_slice, first_one, second_one, intensity)
    back_first_zero = send(rim_zero, 0, 1, first)
    back_second_zero = send(rim_zero, 0, 1, second)
    back_first_one = send(rim_one, 0, 1, first)
    back_second_one = send(rim_one, 0, 1, second)
    mid_one = send(mid_one, 0, 1, same)
    return kernel(
        collect_kernel,
        "collect",
        strip,
        [SMEM] * 5 + [VMEM] * 6,
        0,
        4 << 20,
        (pltpu.VMEM(strip.shape[1:], jnp.float32), pltpu.SemaphoreType.DMA((2 * HALF // CHUNK,))),
        ANY,
    )(
        positions,
        pos_first,
        pos_second,
        first_copy,
        second_copy,
        mid_zero,
        send(back_first_zero, 1, 0, same),
        send(back_second_zero, 1, 0, same),
        back_first_one,
        back_second_one,
        mid_one,
    )


def solution(mesh):
    in_specs = (
        P("cuts", None, "tile", None),
        P(),
        P("tile", None),
        P("tile"),
        P("tile", None, None),
    )
    out_specs = P("cuts", None, "tile", None)
    return jax.shard_map(local, mesh=mesh, in_specs=in_specs, out_specs=out_specs, check_vma=False)
```

```python
import numpy as np
import ml_dtypes

import jax
import jax.numpy as jnp
from jax import lax
from jax.experimental import pallas as pl
from jax.experimental.pallas import tpu as pltpu
from jax.sharding import PartitionSpec as P

WIN = 256
HALF = 128
CHUNK = 64


def split_tables(real_part, imag_part):
    parts = []
    for values in (real_part, imag_part):
        high = values.astype(ml_dtypes.bfloat16)
        low = (values - high.astype(np.float64)).astype(ml_dtypes.bfloat16)
        parts += [high, low]
    return np.stack(parts)


def build_tables():
    index = np.arange(WIN)
    turned = 2.0 * np.pi * ((index[:, None] * index[None, :]) % WIN) / WIN
    dft = (np.cos(turned) - 1j * np.sin(turned)) / np.sqrt(WIN)
    centred = (index + WIN // 2) % WIN - WIN // 2
    phase = np.pi * (centred * centred % (4 * WIN)) / (2 * WIN)
    prop = np.conj(dft) @ ((np.cos(phase) - 1j * np.sin(phase))[:, None] * dft)
    prop = 0.5 * (prop + prop.T)
    return split_tables(dft.real, dft.imag), split_tables(prop.real, prop.imag)


def split(value):
    high = value.astype(jnp.bfloat16)
    low = (value - high.astype(jnp.float32)).astype(jnp.bfloat16)
    return high, low


def dot(left, right):
    return jnp.dot(left, right, preferred_element_type=jnp.float32)


def complex_product(real, imag, table, conjugate, from_left):
    axis = 0 if from_left else 1
    fields = []
    for value in (real, imag):
        high, low = split(value)
        fields.append(jnp.concatenate([high, low, high], axis=axis))
    parts = []
    for which in (0, 2):
        high, low = table[which], table[which + 1]
        parts.append(jnp.concatenate([high, high, low], axis=1 - axis))
    if from_left:
        both = jnp.concatenate(parts, axis=0)
        with_real, with_imag = dot(both, fields[0]), dot(both, fields[1])
        same = with_real[0:WIN], with_imag[0:WIN]
        crossed = with_real[WIN:], with_imag[WIN:]
    else:
        both = jnp.concatenate(fields, axis=0)
        with_cos, with_sin = dot(both, parts[0]), dot(both, parts[1])
        same = with_cos[0:WIN], with_cos[WIN:]
        crossed = with_sin[0:WIN], with_sin[WIN:]
    if conjugate:
        return same[0] + crossed[1], same[1] - crossed[0]
    return same[0] - crossed[1], same[1] + crossed[0]


def sandwich(real, imag, table, conjugate):
    real, imag = complex_product(real, imag, table, conjugate, False)
    return complex_product(real, imag, table, conjugate, True)


def block(number):
    return pl.ds(pl.multiple_of(number * HALF, HALF), HALF)


def cut_piece(strip_ref, column, out_ref):
    first = lax.shift_right_logical(column, 7)
    offset = jnp.bitwise_and(column, HALF - 1)
    lanes = lax.broadcasted_iota(jnp.int32, (HALF, HALF), 1)
    mine = lanes >= offset
    third = jnp.minimum(first + 2, strip_ref.shape[-1] // HALF - 1)
    for part in range(2):
        out_ref[part, :, 0:HALF] = jnp.where(
            mine, strip_ref[0, part, :, block(first)], strip_ref[0, part, :, block(third)]
        )
        out_ref[part, :, HALF:WIN] = strip_ref[0, part, :, block(first + 1)]


def stage_kernel(strip_ref, out_ref, sem):
    copy = pltpu.make_async_copy(strip_ref, out_ref, sem)
    copy.start()
    copy.wait()


def cut_kernel(first_ref, second_ref, strip_ref, to_first_ref, to_second_ref):
    @pl.when(lax.axis_index("cuts") == 1)
    def _():
        for slot in range(2):
            cut_piece(strip_ref, first_ref[slot, 1], to_first_ref.at[slot])
        for slot in range(2):
            cut_piece(strip_ref, second_ref[slot, 1], to_second_ref.at[slot])


def slots_of_core(counts_ref):
    return jnp.where(lax.axis_index("cuts") == 0, counts_ref[0], 0)


def fill_window(pos_ref, slot, strip_ref, first_ref, second_ref, window_ref):
    tile = lax.axis_index("tile")
    odd = jnp.bitwise_and(tile, 1)
    shift_rows = pos_ref[slot, 0] - (tile - 1) * HALF
    column = pos_ref[slot, 1]
    rows = lax.broadcasted_iota(jnp.int32, (HALF, WIN), 0)
    from_first = (1 - 2 * odd) * (rows - shift_rows) >= odd
    for part in range(2):
        window_ref[part, 0:HALF] = jnp.where(
            from_first, first_ref[slot, part], second_ref[slot, part]
        )
    cut_piece(strip_ref, column, window_ref.at[:, HALF:WIN])
    return shift_rows, jnp.bitwise_and(column, HALF - 1)


def enter_kernel(
    pos_ref,
    counts_ref,
    probe_ref,
    table_ref,
    own_ref,
    first_ref,
    second_ref,
    first_copy_ref,
    second_copy_ref,
    wave_ref,
    window_ref,
):
    @pl.loop(0, slots_of_core(counts_ref))
    def _(slot):
        shift_rows, shift_cols = fill_window(pos_ref, slot, own_ref, first_ref, second_ref, window_ref)

        def rolled(part):
            return pltpu.roll(pltpu.roll(probe_ref[part], shift_rows, 0), shift_cols, 1)

        zero_re, zero_im = rolled(0), rolled(1)
        wave_ref[slot, 0, 0] = zero_re
        wave_ref[slot, 0, 1] = zero_im
        cell_re, cell_im = window_ref[0], window_ref[1]
        one_re, one_im = sandwich(
            zero_re * cell_re - zero_im * cell_im,
            zero_re * cell_im + zero_im * cell_re,
            table_ref.at[1],
            False,
        )
        wave_ref[slot, 1, 0] = one_re
        wave_ref[slot, 1, 1] = one_im


def slot_kernel(
    pos_ref,
    counts_ref,
    table_ref,
    wave_ref,
    other_ref,
    first_ref,
    second_ref,
    intensity_ref,
    rim_zero_ref,
    rim_one_ref,
    mid_zero_ref,
    mid_one_ref,
    window_ref,
):
    live_slots = slots_of_core(counts_ref)
    dft_ref, prop_ref = table_ref.at[0], table_ref.at[1]

    @pl.loop(0, live_slots)
    def _(slot):
        fill_window(pos_ref, slot, other_ref, first_ref, second_ref, window_ref)
        cell_re, cell_im = window_ref[0], window_ref[1]
        one_re, one_im = wave_ref[slot, 1, 0], wave_ref[slot, 1, 1]
        far_re, far_im = sandwich(
            one_re * cell_re - one_im * cell_im,
            one_re * cell_im + one_im * cell_re,
            dft_ref,
            False,
        )
        residual = far_re * far_re + far_im * far_im - intensity_ref[slot]
        back_re, back_im = sandwich(far_re * residual, far_im * residual, dft_ref, True)
        for part, value in (
            (0, one_re * back_re + one_im * back_im),
            (1, one_re * back_im - one_im * back_re),
        ):
            rim_one_ref[slot, part] = value[0:HALF]
            mid_one_ref[slot, part] = value[HALF:WIN]
        back_re, back_im = sandwich(
            cell_re * back_re + cell_im * back_im,
            cell_re * back_im - cell_im * back_re,
            prop_ref,
            True,
        )
        zero_re, zero_im = wave_ref[slot, 0, 0], wave_ref[slot, 0, 1]
        for part, value in (
            (0, zero_re * back_re + zero_im * back_im),
            (1, zero_re * back_im - zero_im * back_re),
        ):
            rim_zero_ref[slot, part] = value[0:HALF]
            mid_zero_ref[slot, part] = value[HALF:WIN]

    @pl.when(live_slots == 1)
    def _():
        for ref in (rim_zero_ref, rim_one_ref, mid_zero_ref, mid_one_ref):
            ref[1] = jnp.zeros_like(ref[1])


def add_piece(out_ref, piece_ref, column, keep):
    first = lax.shift_right_logical(column, 7)
    offset = jnp.bitwise_and(column, HALF - 1)
    mine = lax.broadcasted_iota(jnp.int32, (CHUNK, HALF), 1) >= offset
    third = jnp.minimum(first + 2, out_ref.shape[-1] // HALF - 1)
    left = piece_ref[:, 0:HALF]
    right = piece_ref[:, HALF:WIN]
    if keep is not None:
        left = jnp.where(keep, left, 0.0)
        right = jnp.where(keep, right, 0.0)
    out_ref[:, block(first)] += jnp.where(mine, left, 0.0)
    out_ref[:, block(first + 1)] += right
    out_ref[:, block(third)] += jnp.where(mine, 0.0, left)


def collect_kernel(
    pos_ref,
    first_ref,
    second_ref,
    first_copy_ref,
    second_copy_ref,
    mid_zero_ref,
    first_zero_ref,
    second_zero_ref,
    first_one_ref,
    second_one_ref,
    mid_one_ref,
    out_ref,
    sum_ref,
    sem,
):
    core = lax.axis_index("cuts")
    tile = lax.axis_index("tile")
    odd = jnp.bitwise_and(tile, 1)
    rows = lax.broadcasted_iota(jnp.int32, (CHUNK, HALF), 0)

    def gather(mid_ref, *nearby):
        copies = []
        for part in range(2):
            for top in range(0, HALF, CHUNK):
                here = pl.ds(top, CHUNK)
                total = sum_ref.at[part, here]
                total[...] = jnp.zeros(total.shape, jnp.float32)
                for slot in range(2):
                    add_piece(total, mid_ref.at[slot, part, here], pos_ref[slot, 1], None)
                for piece_ref, place_ref, above in nearby:
                    sign = 2 * above - 1
                    for slot in range(2):
                        shift_rows = place_ref[slot, 0] - (tile + sign - 1) * HALF - top
                        keep = sign * (rows - shift_rows) >= 1 - above
                        piece = piece_ref.at[slot, part, here]
                        add_piece(total, piece, place_ref[slot, 1], keep)
                copy = pltpu.make_async_copy(
                    total, out_ref.at[0, part, here], sem.at[len(copies)]
                )
                copy.start()
                copies.append(copy)
        for copy in copies:
            copy.wait()

    @pl.when(core == 0)
    def _():
        gather(
            mid_zero_ref,
            (first_zero_ref, first_copy_ref, odd),
            (second_zero_ref, second_copy_ref, 1 - odd),
        )

    @pl.when(core == 1)
    def _():
        gather(
            mid_one_ref,
            (first_one_ref, first_ref, odd),
            (second_one_ref, second_ref, 1 - odd),
        )


SMEM = pl.BlockSpec(memory_space=pltpu.SMEM)
VMEM = pl.BlockSpec(memory_space=pltpu.VMEM)
ANY = pl.BlockSpec(memory_space=pl.ANY)


LIMIT = 12 << 20


def local(object_slices, probe, positions, counts, intensity):
    tiles = lax.axis_size("tile")

    def first(tile):
        return ((tile + 1) ^ 1) - 1

    def second(tile):
        return tile ^ 1

    def same(tile):
        return tile

    def send(value, source, target, partner):
        pairs = [(tile, partner(tile)) for tile in range(tiles) if 0 <= partner(tile) < tiles]
        pairs = [(source * tiles + one, target * tiles + two) for one, two in pairs]
        return lax.ppermute(value, ("cuts", "tile"), pairs)

    def kernel(body, name, out_shape, in_specs, flops, moved, scratch=(), out_specs=None):
        return pl.pallas_call(
            body,
            out_shape=out_shape,
            in_specs=in_specs,
            out_specs=VMEM if out_specs is None else out_specs,
            scratch_shapes=scratch,
            compiler_params=pltpu.CompilerParams(vmem_limit_bytes=LIMIT),
            cost_estimate=pl.CostEstimate(flops=flops, bytes_accessed=moved, transcendentals=0),
            name=name,
        )

    pieces = jax.ShapeDtypeStruct((2, 2, HALF, WIN), jnp.float32)
    strip = jax.ShapeDtypeStruct(object_slices.shape, jnp.float32)
    window = (pltpu.VMEM((2, WIN, WIN), jnp.float32),)
    tables = jnp.asarray(np.stack(build_tables()))
    other_slice = lax.ppermute(object_slices, "cuts", [(0, 1), (1, 0)])
    pos_first = send(positions, 1, 1, first)
    pos_second = send(positions, 1, 1, second)
    own_slice = kernel(
        stage_kernel, "stage", strip, [ANY], 0, 4 << 20, (pltpu.SemaphoreType.DMA,)
    )(object_slices)

    def cut(name, source):
        return kernel(
            cut_kernel, name, (pieces,) * 2, [SMEM] * 2 + [VMEM], 0, 2 << 20, (), (VMEM,) * 2
        )(pos_first, pos_second, source)

    to_first_zero, to_second_zero = cut("cut_zero", other_slice)
    second_zero = send(to_second_zero, 1, 0, second)
    first_zero = send(to_first_zero, 1, 0, first)
    to_first_one, to_second_one = cut("cut_one", own_slice)
    second_one = send(to_second_one, 1, 0, second)
    first_one = send(to_first_one, 1, 0, first)
    second_copy = send(pos_second, 1, 0, same)
    first_copy = send(pos_first, 1, 0, same)
    wave = kernel(
        enter_kernel,
        "enter",
        jax.ShapeDtypeStruct((2, 2, 2, WIN, WIN), jnp.float32),
        [SMEM] * 2 + [VMEM] * 5 + [ANY] * 2,
        18 * 2 * WIN**3,
        3 << 20,
        window,
    )(positions, counts, probe, tables, own_slice, first_zero, second_zero, first_copy, second_copy)
    rim_zero, rim_one, mid_zero, mid_one = kernel(
        slot_kernel,
        "slot",
        (pieces,) * 4,
        [SMEM] * 2 + [VMEM] * 6,
        54 * 2 * WIN**3,
        6 << 20,
        window,
        (VMEM,) * 4,
    )(positions, counts, tables, wave, other_slice, first_one, second_one, intensity)
    back_first_zero = send(rim_zero, 0, 1, first)
    back_second_zero = send(rim_zero, 0, 1, second)
    back_first_one = send(rim_one, 0, 1, first)
    back_second_one = send(rim_one, 0, 1, second)
    mid_one = send(mid_one, 0, 1, same)
    return kernel(
        collect_kernel,
        "collect",
        strip,
        [SMEM] * 5 + [VMEM] * 6,
        0,
        4 << 20,
        (pltpu.VMEM(strip.shape[1:], jnp.float32), pltpu.SemaphoreType.DMA((2 * HALF // CHUNK,))),
        ANY,
    )(
        positions,
        pos_first,
        pos_second,
        first_copy,
        second_copy,
        mid_zero,
        send(back_first_zero, 1, 0, same),
        send(back_second_zero, 1, 0, same),
        back_first_one,
        back_second_one,
        mid_one,
    )


def solution(mesh):
    in_specs = (
        P("cuts", None, "tile", None),
        P(),
        P("tile", None),
        P("tile"),
        P("tile", None, None),
    )
    out_specs = P("cuts", None, "tile", None)
    return jax.shard_map(local, mesh=mesh, in_specs=in_specs, out_specs=out_specs, check_vma=False)
```

```python
import numpy as np
import ml_dtypes

import jax
import jax.numpy as jnp
from jax import lax
from jax.experimental import pallas as pl
from jax.experimental.pallas import tpu as pltpu
from jax.sharding import PartitionSpec as P

WIN = 256
HALF = 128
CHUNK = 64


def split_tables(real_part, imag_part):
    parts = []
    for values in (real_part, imag_part, -imag_part):
        high = values.astype(ml_dtypes.bfloat16)
        low = (values - high.astype(np.float64)).astype(ml_dtypes.bfloat16)
        parts += [high, low]
    return np.stack(parts)


def build_tables():
    index = np.arange(WIN)
    turned = 2.0 * np.pi * ((index[:, None] * index[None, :]) % WIN) / WIN
    dft = (np.cos(turned) - 1j * np.sin(turned)) / np.sqrt(WIN)
    centred = (index + WIN // 2) % WIN - WIN // 2
    phase = np.pi * (centred * centred % (4 * WIN)) / (2 * WIN)
    prop = np.conj(dft) @ ((np.cos(phase) - 1j * np.sin(phase))[:, None] * dft)
    prop = 0.5 * (prop + prop.T)
    return split_tables(dft.real, dft.imag), split_tables(prop.real, prop.imag)


def split(value):
    high = value.astype(jnp.bfloat16)
    low = (value - high.astype(jnp.float32)).astype(jnp.bfloat16)
    return high, low


def dot(left, right):
    return jnp.dot(left, right, preferred_element_type=jnp.float32)


def terms_of(real, imag):
    real_high, real_low = split(real)
    imag_high, imag_low = split(imag)
    return [real_high, real_low, real_high, imag_high, imag_low, imag_high]


def sandwich(real, imag, table, conjugate):
    plus, minus = (2, 1) if conjugate else (1, 2)

    def weights(which, rows):
        high, low = table[2 * which, rows], table[2 * which + 1, rows]
        return [high, high, low]

    every = slice(0, WIN)
    halves = [slice(0, HALF), slice(HALF, WIN)]
    right = [
        jnp.concatenate(weights(0, every) + weights(minus, every), axis=0),
        jnp.concatenate(weights(plus, every) + weights(0, every), axis=0),
    ]
    middle = []
    for rows in halves:
        field = jnp.concatenate(terms_of(real[rows], imag[rows]), axis=1)
        middle.append(terms_of(dot(field, right[0]), dot(field, right[1])))
    stacked = jnp.concatenate(
        [jnp.concatenate(pair, axis=0) for pair in zip(*middle)], axis=0
    )
    results = [[], []]
    for rows in halves:
        left = jnp.concatenate(weights(0, rows) + weights(minus, rows), axis=1)
        results[0].append(dot(left, stacked))
        left = jnp.concatenate(weights(plus, rows) + weights(0, rows), axis=1)
        results[1].append(dot(left, stacked))
    return [jnp.concatenate(parts, axis=0) for parts in results]


def block(number):
    return pl.ds(pl.multiple_of(number * HALF, HALF), HALF)


def cut_piece(strip_ref, column, out_ref):
    first = lax.shift_right_logical(column, 7)
    offset = jnp.bitwise_and(column, HALF - 1)
    lanes = lax.broadcasted_iota(jnp.int32, (HALF, HALF), 1)
    mine = lanes >= offset
    third = jnp.minimum(first + 2, strip_ref.shape[-1] // HALF - 1)
    for part in range(2):
        out_ref[part, :, 0:HALF] = jnp.where(
            mine, strip_ref[0, part, :, block(first)], strip_ref[0, part, :, block(third)]
        )
        out_ref[part, :, HALF:WIN] = strip_ref[0, part, :, block(first + 1)]


def stage_kernel(strip_ref, out_ref, sem):
    copy = pltpu.make_async_copy(strip_ref, out_ref, sem)
    copy.start()
    copy.wait()


def cut_kernel(first_ref, second_ref, strip_ref, to_first_ref, to_second_ref):
    @pl.when(lax.axis_index("cuts") == 1)
    def _():
        for slot in range(2):
            cut_piece(strip_ref, first_ref[slot, 1], to_first_ref.at[slot])
        for slot in range(2):
            cut_piece(strip_ref, second_ref[slot, 1], to_second_ref.at[slot])


def slots_of_core(counts_ref):
    return jnp.where(lax.axis_index("cuts") == 0, counts_ref[0], 0)


def fill_window(pos_ref, slot, strip_ref, first_ref, second_ref, window_ref):
    tile = lax.axis_index("tile")
    odd = jnp.bitwise_and(tile, 1)
    shift_rows = pos_ref[slot, 0] - (tile - 1) * HALF
    column = pos_ref[slot, 1]
    rows = lax.broadcasted_iota(jnp.int32, (HALF, WIN), 0)
    from_first = (1 - 2 * odd) * (rows - shift_rows) >= odd
    for part in range(2):
        window_ref[part, 0:HALF] = jnp.where(
            from_first, first_ref[slot, part], second_ref[slot, part]
        )
    cut_piece(strip_ref, column, window_ref.at[:, HALF:WIN])
    return shift_rows, jnp.bitwise_and(column, HALF - 1)


def enter_kernel(
    pos_ref,
    counts_ref,
    probe_ref,
    table_ref,
    own_ref,
    first_ref,
    second_ref,
    first_copy_ref,
    second_copy_ref,
    wave_ref,
    window_ref,
):
    @pl.loop(0, slots_of_core(counts_ref))
    def _(slot):
        shift_rows, shift_cols = fill_window(pos_ref, slot, own_ref, first_ref, second_ref, window_ref)

        def rolled(part):
            return pltpu.roll(pltpu.roll(probe_ref[part], shift_rows, 0), shift_cols, 1)

        zero_re, zero_im = rolled(0), rolled(1)
        wave_ref[slot, 0, 0] = zero_re
        wave_ref[slot, 0, 1] = zero_im
        cell_re, cell_im = window_ref[0], window_ref[1]
        one_re, one_im = sandwich(
            zero_re * cell_re - zero_im * cell_im,
            zero_re * cell_im + zero_im * cell_re,
            table_ref.at[1],
            False,
        )
        wave_ref[slot, 1, 0] = one_re
        wave_ref[slot, 1, 1] = one_im


def slot_kernel(
    pos_ref,
    counts_ref,
    table_ref,
    wave_ref,
    other_ref,
    first_ref,
    second_ref,
    intensity_ref,
    rim_zero_ref,
    rim_one_ref,
    mid_zero_ref,
    mid_one_ref,
    window_ref,
):
    live_slots = slots_of_core(counts_ref)
    dft_ref, prop_ref = table_ref.at[0], table_ref.at[1]

    @pl.loop(0, live_slots)
    def _(slot):
        fill_window(pos_ref, slot, other_ref, first_ref, second_ref, window_ref)
        cell_re, cell_im = window_ref[0], window_ref[1]
        one_re, one_im = wave_ref[slot, 1, 0], wave_ref[slot, 1, 1]
        far_re, far_im = sandwich(
            one_re * cell_re - one_im * cell_im,
            one_re * cell_im + one_im * cell_re,
            dft_ref,
            False,
        )
        residual = far_re * far_re + far_im * far_im - intensity_ref[slot]
        back_re, back_im = sandwich(far_re * residual, far_im * residual, dft_ref, True)
        for part, value in (
            (0, one_re * back_re + one_im * back_im),
            (1, one_re * back_im - one_im * back_re),
        ):
            rim_one_ref[slot, part] = value[0:HALF]
            mid_one_ref[slot, part] = value[HALF:WIN]
        back_re, back_im = sandwich(
            cell_re * back_re + cell_im * back_im,
            cell_re * back_im - cell_im * back_re,
            prop_ref,
            True,
        )
        zero_re, zero_im = wave_ref[slot, 0, 0], wave_ref[slot, 0, 1]
        for part, value in (
            (0, zero_re * back_re + zero_im * back_im),
            (1, zero_re * back_im - zero_im * back_re),
        ):
            rim_zero_ref[slot, part] = value[0:HALF]
            mid_zero_ref[slot, part] = value[HALF:WIN]

    @pl.when(live_slots == 1)
    def _():
        for ref in (rim_zero_ref, rim_one_ref, mid_zero_ref, mid_one_ref):
            ref[1] = jnp.zeros_like(ref[1])


def add_piece(out_ref, piece_ref, column, keep):
    first = lax.shift_right_logical(column, 7)
    offset = jnp.bitwise_and(column, HALF - 1)
    mine = lax.broadcasted_iota(jnp.int32, (CHUNK, HALF), 1) >= offset
    third = jnp.minimum(first + 2, out_ref.shape[-1] // HALF - 1)
    left = piece_ref[:, 0:HALF]
    right = piece_ref[:, HALF:WIN]
    if keep is not None:
        left = jnp.where(keep, left, 0.0)
        right = jnp.where(keep, right, 0.0)
    out_ref[:, block(first)] += jnp.where(mine, left, 0.0)
    out_ref[:, block(first + 1)] += right
    out_ref[:, block(third)] += jnp.where(mine, 0.0, left)


def collect_kernel(
    pos_ref,
    first_ref,
    second_ref,
    first_copy_ref,
    second_copy_ref,
    mid_zero_ref,
    first_zero_ref,
    second_zero_ref,
    first_one_ref,
    second_one_ref,
    mid_one_ref,
    out_ref,
    sum_ref,
    sem,
):
    core = lax.axis_index("cuts")
    tile = lax.axis_index("tile")
    odd = jnp.bitwise_and(tile, 1)
    rows = lax.broadcasted_iota(jnp.int32, (CHUNK, HALF), 0)

    def gather(mid_ref, *nearby):
        copies = []
        for part in range(2):
            for top in range(0, HALF, CHUNK):
                here = pl.ds(top, CHUNK)
                total = sum_ref.at[part, here]
                total[...] = jnp.zeros(total.shape, jnp.float32)
                for slot in range(2):
                    add_piece(total, mid_ref.at[slot, part, here], pos_ref[slot, 1], None)
                for piece_ref, place_ref, above in nearby:
                    sign = 2 * above - 1
                    for slot in range(2):
                        shift_rows = place_ref[slot, 0] - (tile + sign - 1) * HALF - top
                        keep = sign * (rows - shift_rows) >= 1 - above
                        piece = piece_ref.at[slot, part, here]
                        add_piece(total, piece, place_ref[slot, 1], keep)
                copy = pltpu.make_async_copy(
                    total, out_ref.at[0, part, here], sem.at[len(copies)]
                )
                copy.start()
                copies.append(copy)
        for copy in copies:
            copy.wait()

    @pl.when(core == 0)
    def _():
        gather(
            mid_zero_ref,
            (first_zero_ref, first_copy_ref, odd),
            (second_zero_ref, second_copy_ref, 1 - odd),
        )

    @pl.when(core == 1)
    def _():
        gather(
            mid_one_ref,
            (first_one_ref, first_ref, odd),
            (second_one_ref, second_ref, 1 - odd),
        )


SMEM = pl.BlockSpec(memory_space=pltpu.SMEM)
VMEM = pl.BlockSpec(memory_space=pltpu.VMEM)
ANY = pl.BlockSpec(memory_space=pl.ANY)


LIMIT = 12 << 20


def local(object_slices, probe, positions, counts, intensity):
    tiles = lax.axis_size("tile")

    def first(tile):
        return ((tile + 1) ^ 1) - 1

    def second(tile):
        return tile ^ 1

    def same(tile):
        return tile

    def send(value, source, target, partner):
        pairs = [(tile, partner(tile)) for tile in range(tiles) if 0 <= partner(tile) < tiles]
        pairs = [(source * tiles + one, target * tiles + two) for one, two in pairs]
        return lax.ppermute(value, ("cuts", "tile"), pairs)

    def kernel(body, name, out_shape, in_specs, flops, moved, scratch=(), out_specs=None):
        return pl.pallas_call(
            body,
            out_shape=out_shape,
            in_specs=in_specs,
            out_specs=VMEM if out_specs is None else out_specs,
            scratch_shapes=scratch,
            compiler_params=pltpu.CompilerParams(vmem_limit_bytes=LIMIT),
            cost_estimate=pl.CostEstimate(flops=flops, bytes_accessed=moved, transcendentals=0),
            name=name,
        )

    pieces = jax.ShapeDtypeStruct((2, 2, HALF, WIN), jnp.float32)
    strip = jax.ShapeDtypeStruct(object_slices.shape, jnp.float32)
    window = (pltpu.VMEM((2, WIN, WIN), jnp.float32),)
    tables = jnp.asarray(np.stack(build_tables()))
    other_slice = lax.ppermute(object_slices, "cuts", [(0, 1), (1, 0)])
    pos_first = send(positions, 1, 1, first)
    pos_second = send(positions, 1, 1, second)
    own_slice = kernel(
        stage_kernel, "stage", strip, [ANY], 0, 4 << 20, (pltpu.SemaphoreType.DMA,)
    )(object_slices)

    def cut(name, source):
        return kernel(
            cut_kernel, name, (pieces,) * 2, [SMEM] * 2 + [VMEM], 0, 2 << 20, (), (VMEM,) * 2
        )(pos_first, pos_second, source)

    to_first_zero, to_second_zero = cut("cut_zero", other_slice)
    second_zero = send(to_second_zero, 1, 0, second)
    first_zero = send(to_first_zero, 1, 0, first)
    to_first_one, to_second_one = cut("cut_one", own_slice)
    second_one = send(to_second_one, 1, 0, second)
    first_one = send(to_first_one, 1, 0, first)
    second_copy = send(pos_second, 1, 0, same)
    first_copy = send(pos_first, 1, 0, same)
    wave = kernel(
        enter_kernel,
        "enter",
        jax.ShapeDtypeStruct((2, 2, 2, WIN, WIN), jnp.float32),
        [SMEM] * 2 + [VMEM] * 5 + [ANY] * 2,
        18 * 2 * WIN**3,
        3 << 20,
        window,
    )(positions, counts, probe, tables, own_slice, first_zero, second_zero, first_copy, second_copy)
    rim_zero, rim_one, mid_zero, mid_one = kernel(
        slot_kernel,
        "slot",
        (pieces,) * 4,
        [SMEM] * 2 + [VMEM] * 6,
        54 * 2 * WIN**3,
        6 << 20,
        window,
        (VMEM,) * 4,
    )(positions, counts, tables, wave, other_slice, first_one, second_one, intensity)
    back_first_zero = send(rim_zero, 0, 1, first)
    back_second_zero = send(rim_zero, 0, 1, second)
    back_first_one = send(rim_one, 0, 1, first)
    back_second_one = send(rim_one, 0, 1, second)
    mid_one = send(mid_one, 0, 1, same)
    return kernel(
        collect_kernel,
        "collect",
        strip,
        [SMEM] * 5 + [VMEM] * 6,
        0,
        4 << 20,
        (pltpu.VMEM(strip.shape[1:], jnp.float32), pltpu.SemaphoreType.DMA((2 * HALF // CHUNK,))),
        ANY,
    )(
        positions,
        pos_first,
        pos_second,
        first_copy,
        second_copy,
        mid_zero,
        send(back_first_zero, 1, 0, same),
        send(back_second_zero, 1, 0, same),
        back_first_one,
        back_second_one,
        mid_one,
    )


def solution(mesh):
    in_specs = (
        P("cuts", None, "tile", None),
        P(),
        P("tile", None),
        P("tile"),
        P("tile", None, None),
    )
    out_specs = P("cuts", None, "tile", None)
    return jax.shard_map(local, mesh=mesh, in_specs=in_specs, out_specs=out_specs, check_vma=False)
```

```python
import numpy as np
import ml_dtypes

import jax
import jax.numpy as jnp
from jax import lax
from jax.experimental import pallas as pl
from jax.experimental.pallas import tpu as pltpu
from jax.sharding import PartitionSpec as P

WIN = 256
HALF = 128
CHUNK = 64


def split_tables(real_part, imag_part):
    parts = []
    for values in (real_part, imag_part, -imag_part):
        high = values.astype(ml_dtypes.bfloat16)
        low = (values - high.astype(np.float64)).astype(ml_dtypes.bfloat16)
        parts += [high, low]
    return np.stack(parts)


def build_tables():
    index = np.arange(WIN)
    turned = 2.0 * np.pi * ((index[:, None] * index[None, :]) % WIN) / WIN
    dft = (np.cos(turned) - 1j * np.sin(turned)) / np.sqrt(WIN)
    centred = (index + WIN // 2) % WIN - WIN // 2
    phase = np.pi * (centred * centred % (4 * WIN)) / (2 * WIN)
    prop = np.conj(dft) @ ((np.cos(phase) - 1j * np.sin(phase))[:, None] * dft)
    prop = 0.5 * (prop + prop.T)
    return split_tables(dft.real, dft.imag), split_tables(prop.real, prop.imag)


def split(value):
    high = value.astype(jnp.bfloat16)
    low = (value - high.astype(jnp.float32)).astype(jnp.bfloat16)
    return high, low


def dot(left, right):
    return jnp.dot(left, right, preferred_element_type=jnp.float32)


def complex_product(real, imag, table, conjugate, from_left):
    real_high, real_low = split(real)
    imag_high, imag_low = split(imag)
    fields = [real_high, real_low, real_high, imag_high, imag_low, imag_high]

    def terms(which):
        return [table[2 * which], table[2 * which], table[2 * which + 1]]

    plus, minus = (2, 1) if conjugate else (1, 2)
    results = []
    for parts in (terms(0) + terms(minus), terms(plus) + terms(0)):
        if from_left:
            left, right = jnp.concatenate(parts, axis=1), jnp.concatenate(fields, axis=0)
        else:
            left, right = jnp.concatenate(fields, axis=1), jnp.concatenate(parts, axis=0)
        results.append(dot(left, right))
    return results


def sandwich(real, imag, table, conjugate):
    real, imag = complex_product(real, imag, table, conjugate, False)
    return complex_product(real, imag, table, conjugate, True)


def block(number):
    return pl.ds(pl.multiple_of(number * HALF, HALF), HALF)


def entry(ref, slot, which):
    rows = lax.broadcasted_iota(jnp.int32, (2, 2), 0)
    columns = lax.broadcasted_iota(jnp.int32, (2, 2), 1)
    values = ref[...].astype(jnp.float32)
    chosen = jnp.where((rows == slot) & (columns == which), values, 0.0)
    return jnp.sum(chosen).astype(jnp.int32)


def cut_piece(strip_ref, column, out_ref):
    first = lax.shift_right_logical(column, 7)
    offset = jnp.bitwise_and(column, HALF - 1)
    lanes = lax.broadcasted_iota(jnp.int32, (HALF, HALF), 1)
    mine = lanes >= offset
    third = jnp.minimum(first + 2, strip_ref.shape[-1] // HALF - 1)
    for part in range(2):
        out_ref[part, :, 0:HALF] = jnp.where(
            mine, strip_ref[0, part, :, block(first)], strip_ref[0, part, :, block(third)]
        )
        out_ref[part, :, HALF:WIN] = strip_ref[0, part, :, block(first + 1)]


def stage_kernel(strip_ref, out_ref, sem):
    copy = pltpu.make_async_copy(strip_ref, out_ref, sem)
    copy.start()
    copy.wait()


def cut_kernel(first_ref, second_ref, strip_ref, to_first_ref, to_second_ref):
    @pl.when(lax.axis_index("cuts") == 1)
    def _():
        for slot in range(2):
            cut_piece(strip_ref, entry(first_ref, slot, 1), to_first_ref.at[slot])
        for slot in range(2):
            cut_piece(strip_ref, entry(second_ref, slot, 1), to_second_ref.at[slot])


def slots_of_core(counts_ref):
    return jnp.where(lax.axis_index("cuts") == 0, counts_ref[0], 0)


def fill_window(pos_ref, slot, strip_ref, first_ref, second_ref, window_ref):
    tile = lax.axis_index("tile")
    odd = jnp.bitwise_and(tile, 1)
    shift_rows = entry(pos_ref, slot, 0) - (tile - 1) * HALF
    column = entry(pos_ref, slot, 1)
    rows = lax.broadcasted_iota(jnp.int32, (HALF, WIN), 0)
    from_first = (1 - 2 * odd) * (rows - shift_rows) >= odd
    for part in range(2):
        window_ref[part, 0:HALF] = jnp.where(
            from_first, first_ref[slot, part], second_ref[slot, part]
        )
    cut_piece(strip_ref, column, window_ref.at[:, HALF:WIN])
    return shift_rows, jnp.bitwise_and(column, HALF - 1)


def enter_kernel(
    pos_ref,
    counts_ref,
    probe_ref,
    table_ref,
    own_ref,
    first_ref,
    second_ref,
    first_copy_ref,
    second_copy_ref,
    wave_ref,
    window_ref,
):
    @pl.loop(0, slots_of_core(counts_ref))
    def _(slot):
        shift_rows, shift_cols = fill_window(pos_ref, slot, own_ref, first_ref, second_ref, window_ref)

        def rolled(part):
            return pltpu.roll(pltpu.roll(probe_ref[part], shift_rows, 0), shift_cols, 1)

        zero_re, zero_im = rolled(0), rolled(1)
        wave_ref[slot, 0, 0] = zero_re
        wave_ref[slot, 0, 1] = zero_im
        cell_re, cell_im = window_ref[0], window_ref[1]
        one_re, one_im = sandwich(
            zero_re * cell_re - zero_im * cell_im,
            zero_re * cell_im + zero_im * cell_re,
            table_ref.at[1],
            False,
        )
        wave_ref[slot, 1, 0] = one_re
        wave_ref[slot, 1, 1] = one_im


def slot_kernel(
    pos_ref,
    counts_ref,
    table_ref,
    wave_ref,
    other_ref,
    first_ref,
    second_ref,
    intensity_ref,
    rim_zero_ref,
    rim_one_ref,
    mid_zero_ref,
    mid_one_ref,
    window_ref,
):
    live_slots = slots_of_core(counts_ref)
    dft_ref, prop_ref = table_ref.at[0], table_ref.at[1]

    @pl.loop(0, live_slots)
    def _(slot):
        fill_window(pos_ref, slot, other_ref, first_ref, second_ref, window_ref)
        cell_re, cell_im = window_ref[0], window_ref[1]
        one_re, one_im = wave_ref[slot, 1, 0], wave_ref[slot, 1, 1]
        far_re, far_im = sandwich(
            one_re * cell_re - one_im * cell_im,
            one_re * cell_im + one_im * cell_re,
            dft_ref,
            False,
        )
        residual = far_re * far_re + far_im * far_im - intensity_ref[slot]
        back_re, back_im = sandwich(far_re * residual, far_im * residual, dft_ref, True)
        for part, value in (
            (0, one_re * back_re + one_im * back_im),
            (1, one_re * back_im - one_im * back_re),
        ):
            rim_one_ref[slot, part] = value[0:HALF]
            mid_one_ref[slot, part] = value[HALF:WIN]
        back_re, back_im = sandwich(
            cell_re * back_re + cell_im * back_im,
            cell_re * back_im - cell_im * back_re,
            prop_ref,
            True,
        )
        zero_re, zero_im = wave_ref[slot, 0, 0], wave_ref[slot, 0, 1]
        for part, value in (
            (0, zero_re * back_re + zero_im * back_im),
            (1, zero_re * back_im - zero_im * back_re),
        ):
            rim_zero_ref[slot, part] = value[0:HALF]
            mid_zero_ref[slot, part] = value[HALF:WIN]

    @pl.when(live_slots == 1)
    def _():
        for ref in (rim_zero_ref, rim_one_ref, mid_zero_ref, mid_one_ref):
            ref[1] = jnp.zeros_like(ref[1])


def add_piece(out_ref, piece_ref, column, keep):
    first = lax.shift_right_logical(column, 7)
    offset = jnp.bitwise_and(column, HALF - 1)
    mine = lax.broadcasted_iota(jnp.int32, (CHUNK, HALF), 1) >= offset
    third = jnp.minimum(first + 2, out_ref.shape[-1] // HALF - 1)
    left = piece_ref[:, 0:HALF]
    right = piece_ref[:, HALF:WIN]
    if keep is not None:
        left = jnp.where(keep, left, 0.0)
        right = jnp.where(keep, right, 0.0)
    out_ref[:, block(first)] += jnp.where(mine, left, 0.0)
    out_ref[:, block(first + 1)] += right
    out_ref[:, block(third)] += jnp.where(mine, 0.0, left)


def collect_kernel(
    pos_ref,
    first_ref,
    second_ref,
    first_copy_ref,
    second_copy_ref,
    mid_zero_ref,
    first_zero_ref,
    second_zero_ref,
    first_one_ref,
    second_one_ref,
    mid_one_ref,
    out_ref,
    sum_ref,
    sem,
):
    core = lax.axis_index("cuts")
    tile = lax.axis_index("tile")
    odd = jnp.bitwise_and(tile, 1)
    rows = lax.broadcasted_iota(jnp.int32, (CHUNK, HALF), 0)

    def gather(mid_ref, *nearby):
        copies = []
        columns = [entry(pos_ref, slot, 1) for slot in range(2)]
        places = [
            [(entry(place_ref, slot, 0), entry(place_ref, slot, 1)) for slot in range(2)]
            for _, place_ref, _ in nearby
        ]
        for part in range(2):
            for top in range(0, HALF, CHUNK):
                here = pl.ds(top, CHUNK)
                total = sum_ref.at[part, here]
                total[...] = jnp.zeros(total.shape, jnp.float32)
                for slot in range(2):
                    add_piece(total, mid_ref.at[slot, part, here], columns[slot], None)
                for (piece_ref, _, above), place in zip(nearby, places):
                    sign = 2 * above - 1
                    for slot in range(2):
                        shift_rows = place[slot][0] - (tile + sign - 1) * HALF - top
                        keep = sign * (rows - shift_rows) >= 1 - above
                        piece = piece_ref.at[slot, part, here]
                        add_piece(total, piece, place[slot][1], keep)
                copy = pltpu.make_async_copy(
                    total, out_ref.at[0, part, here], sem.at[len(copies)]
                )
                copy.start()
                copies.append(copy)
        for copy in copies:
            copy.wait()

    @pl.when(core == 0)
    def _():
        gather(
            mid_zero_ref,
            (first_zero_ref, first_copy_ref, odd),
            (second_zero_ref, second_copy_ref, 1 - odd),
        )

    @pl.when(core == 1)
    def _():
        gather(
            mid_one_ref,
            (first_one_ref, first_ref, odd),
            (second_one_ref, second_ref, 1 - odd),
        )


SMEM = pl.BlockSpec(memory_space=pltpu.SMEM)
VMEM = pl.BlockSpec(memory_space=pltpu.VMEM)
ANY = pl.BlockSpec(memory_space=pl.ANY)


LIMIT = 12 << 20


def local(object_slices, probe, positions, counts, intensity):
    tiles = lax.axis_size("tile")

    def first(tile):
        return ((tile + 1) ^ 1) - 1

    def second(tile):
        return tile ^ 1

    def same(tile):
        return tile

    def send(value, source, target, partner):
        pairs = [(tile, partner(tile)) for tile in range(tiles) if 0 <= partner(tile) < tiles]
        pairs = [(source * tiles + one, target * tiles + two) for one, two in pairs]
        return lax.ppermute(value, ("cuts", "tile"), pairs)

    def kernel(body, name, out_shape, in_specs, flops, moved, scratch=(), out_specs=None):
        return pl.pallas_call(
            body,
            out_shape=out_shape,
            in_specs=in_specs,
            out_specs=VMEM if out_specs is None else out_specs,
            scratch_shapes=scratch,
            compiler_params=pltpu.CompilerParams(vmem_limit_bytes=LIMIT),
            cost_estimate=pl.CostEstimate(flops=flops, bytes_accessed=moved, transcendentals=0),
            name=name,
        )

    pieces = jax.ShapeDtypeStruct((2, 2, HALF, WIN), jnp.float32)
    strip = jax.ShapeDtypeStruct(object_slices.shape, jnp.float32)
    window = (pltpu.VMEM((2, WIN, WIN), jnp.float32),)
    tables = jnp.asarray(np.stack(build_tables()))
    other_slice = lax.ppermute(object_slices, "cuts", [(0, 1), (1, 0)])
    pos_first = send(positions, 1, 1, first)
    pos_second = send(positions, 1, 1, second)
    own_slice = kernel(
        stage_kernel, "stage", strip, [ANY], 0, 4 << 20, (pltpu.SemaphoreType.DMA,)
    )(object_slices)

    def cut(name, source):
        return kernel(
            cut_kernel, name, (pieces,) * 2, [VMEM] * 2 + [VMEM], 0, 2 << 20, (), (VMEM,) * 2
        )(pos_first, pos_second, source)

    to_first_zero, to_second_zero = cut("cut_zero", other_slice)
    second_zero = send(to_second_zero, 1, 0, second)
    first_zero = send(to_first_zero, 1, 0, first)
    to_first_one, to_second_one = cut("cut_one", own_slice)
    second_one = send(to_second_one, 1, 0, second)
    first_one = send(to_first_one, 1, 0, first)
    second_copy = send(pos_second, 1, 0, same)
    first_copy = send(pos_first, 1, 0, same)
    wave = kernel(
        enter_kernel,
        "enter",
        jax.ShapeDtypeStruct((2, 2, 2, WIN, WIN), jnp.float32),
        [VMEM, SMEM] + [VMEM] * 5 + [ANY] * 2,
        18 * 2 * WIN**3,
        3 << 20,
        window,
    )(positions, counts, probe, tables, own_slice, first_zero, second_zero, first_copy, second_copy)
    rim_zero, rim_one, mid_zero, mid_one = kernel(
        slot_kernel,
        "slot",
        (pieces,) * 4,
        [VMEM, SMEM] + [VMEM] * 6,
        54 * 2 * WIN**3,
        6 << 20,
        window,
        (VMEM,) * 4,
    )(positions, counts, tables, wave, other_slice, first_one, second_one, intensity)
    back_first_zero = send(rim_zero, 0, 1, first)
    back_second_zero = send(rim_zero, 0, 1, second)
    back_first_one = send(rim_one, 0, 1, first)
    back_second_one = send(rim_one, 0, 1, second)
    mid_one = send(mid_one, 0, 1, same)
    return kernel(
        collect_kernel,
        "collect",
        strip,
        [VMEM] * 11,
        0,
        4 << 20,
        (pltpu.VMEM(strip.shape[1:], jnp.float32), pltpu.SemaphoreType.DMA((2 * HALF // CHUNK,))),
        ANY,
    )(
        positions,
        pos_first,
        pos_second,
        first_copy,
        second_copy,
        mid_zero,
        send(back_first_zero, 1, 0, same),
        send(back_second_zero, 1, 0, same),
        back_first_one,
        back_second_one,
        mid_one,
    )


def solution(mesh):
    in_specs = (
        P("cuts", None, "tile", None),
        P(),
        P("tile", None),
        P("tile"),
        P("tile", None, None),
    )
    out_specs = P("cuts", None, "tile", None)
    return jax.shard_map(local, mesh=mesh, in_specs=in_specs, out_specs=out_specs, check_vma=False)
```

```python
import numpy as np
import ml_dtypes

import jax
import jax.numpy as jnp
from jax import lax
from jax.experimental import pallas as pl
from jax.experimental.pallas import tpu as pltpu
from jax.sharding import PartitionSpec as P

WIN = 256
HALF = 128
CHUNK = 32


def split_tables(real_part, imag_part):
    parts = []
    for values in (real_part, imag_part, -imag_part):
        high = values.astype(ml_dtypes.bfloat16)
        low = (values - high.astype(np.float64)).astype(ml_dtypes.bfloat16)
        parts += [high, low]
    return np.stack(parts)


def build_tables():
    index = np.arange(WIN)
    turned = 2.0 * np.pi * ((index[:, None] * index[None, :]) % WIN) / WIN
    dft = (np.cos(turned) - 1j * np.sin(turned)) / np.sqrt(WIN)
    centred = (index + WIN // 2) % WIN - WIN // 2
    phase = np.pi * (centred * centred % (4 * WIN)) / (2 * WIN)
    prop = np.conj(dft) @ ((np.cos(phase) - 1j * np.sin(phase))[:, None] * dft)
    prop = 0.5 * (prop + prop.T)
    return split_tables(dft.real, dft.imag), split_tables(prop.real, prop.imag)


def split(value):
    high = value.astype(jnp.bfloat16)
    low = (value - high.astype(jnp.float32)).astype(jnp.bfloat16)
    return high, low


def dot(left, right):
    return jnp.dot(left, right, preferred_element_type=jnp.float32)


def complex_product(real, imag, table, conjugate, from_left):
    real_high, real_low = split(real)
    imag_high, imag_low = split(imag)
    fields = [real_high, real_low, real_high, imag_high, imag_low, imag_high]

    def terms(which):
        return [table[2 * which], table[2 * which], table[2 * which + 1]]

    plus, minus = (2, 1) if conjugate else (1, 2)
    results = []
    for parts in (terms(0) + terms(minus), terms(plus) + terms(0)):
        if from_left:
            left, right = jnp.concatenate(parts, axis=1), jnp.concatenate(fields, axis=0)
        else:
            left, right = jnp.concatenate(fields, axis=1), jnp.concatenate(parts, axis=0)
        results.append(dot(left, right))
    return results


def sandwich(real, imag, table, conjugate):
    real, imag = complex_product(real, imag, table, conjugate, False)
    return complex_product(real, imag, table, conjugate, True)


def block(number):
    return pl.ds(pl.multiple_of(number * HALF, HALF), HALF)


def entry(ref, slot, which):
    rows = lax.broadcasted_iota(jnp.int32, (2, 2), 0)
    columns = lax.broadcasted_iota(jnp.int32, (2, 2), 1)
    values = ref[...].astype(jnp.float32)
    chosen = jnp.where((rows == slot) & (columns == which), values, 0.0)
    return jnp.sum(chosen).astype(jnp.int32)


def cut_piece(strip_ref, column, out_ref):
    first = lax.shift_right_logical(column, 7)
    offset = jnp.bitwise_and(column, HALF - 1)
    lanes = lax.broadcasted_iota(jnp.int32, (HALF, HALF), 1)
    mine = lanes >= offset
    third = jnp.minimum(first + 2, strip_ref.shape[-1] // HALF - 1)
    for part in range(2):
        out_ref[part, :, 0:HALF] = jnp.where(
            mine, strip_ref[0, part, :, block(first)], strip_ref[0, part, :, block(third)]
        )
        out_ref[part, :, HALF:WIN] = strip_ref[0, part, :, block(first + 1)]


def stage_kernel(strip_ref, out_ref, sem):
    copy = pltpu.make_async_copy(strip_ref, out_ref, sem)
    copy.start()
    copy.wait()


def cut_kernel(first_ref, second_ref, strip_ref, to_first_ref, to_second_ref):
    @pl.when(lax.axis_index("cuts") == 1)
    def _():
        for slot in range(2):
            cut_piece(strip_ref, entry(first_ref, slot, 1), to_first_ref.at[slot])
        for slot in range(2):
            cut_piece(strip_ref, entry(second_ref, slot, 1), to_second_ref.at[slot])


def slots_of_core(counts_ref):
    return jnp.where(lax.axis_index("cuts") == 0, counts_ref[0], 0)


def fill_window(pos_ref, slot, strip_ref, first_ref, second_ref, window_ref):
    tile = lax.axis_index("tile")
    odd = jnp.bitwise_and(tile, 1)
    shift_rows = entry(pos_ref, slot, 0) - (tile - 1) * HALF
    column = entry(pos_ref, slot, 1)
    rows = lax.broadcasted_iota(jnp.int32, (HALF, WIN), 0)
    from_first = (1 - 2 * odd) * (rows - shift_rows) >= odd
    for part in range(2):
        window_ref[part, 0:HALF] = jnp.where(
            from_first, first_ref[slot, part], second_ref[slot, part]
        )
    cut_piece(strip_ref, column, window_ref.at[:, HALF:WIN])
    return shift_rows, jnp.bitwise_and(column, HALF - 1)


def enter_kernel(
    pos_ref,
    counts_ref,
    probe_ref,
    table_ref,
    own_ref,
    first_ref,
    second_ref,
    first_copy_ref,
    second_copy_ref,
    wave_ref,
    window_ref,
):
    @pl.loop(0, slots_of_core(counts_ref))
    def _(slot):
        shift_rows, shift_cols = fill_window(pos_ref, slot, own_ref, first_ref, second_ref, window_ref)

        def rolled(part):
            return pltpu.roll(pltpu.roll(probe_ref[part], shift_rows, 0), shift_cols, 1)

        zero_re, zero_im = rolled(0), rolled(1)
        wave_ref[slot, 0, 0] = zero_re
        wave_ref[slot, 0, 1] = zero_im
        cell_re, cell_im = window_ref[0], window_ref[1]
        one_re, one_im = sandwich(
            zero_re * cell_re - zero_im * cell_im,
            zero_re * cell_im + zero_im * cell_re,
            table_ref.at[1],
            False,
        )
        wave_ref[slot, 1, 0] = one_re
        wave_ref[slot, 1, 1] = one_im


def slot_kernel(
    pos_ref,
    counts_ref,
    table_ref,
    wave_ref,
    other_ref,
    first_ref,
    second_ref,
    intensity_ref,
    rim_zero_ref,
    rim_one_ref,
    mid_zero_ref,
    mid_one_ref,
    window_ref,
):
    live_slots = slots_of_core(counts_ref)
    dft_ref, prop_ref = table_ref.at[0], table_ref.at[1]

    @pl.loop(0, live_slots)
    def _(slot):
        fill_window(pos_ref, slot, other_ref, first_ref, second_ref, window_ref)
        cell_re, cell_im = window_ref[0], window_ref[1]
        one_re, one_im = wave_ref[slot, 1, 0], wave_ref[slot, 1, 1]
        far_re, far_im = sandwich(
            one_re * cell_re - one_im * cell_im,
            one_re * cell_im + one_im * cell_re,
            dft_ref,
            False,
        )
        residual = far_re * far_re + far_im * far_im - intensity_ref[slot]
        back_re, back_im = sandwich(far_re * residual, far_im * residual, dft_ref, True)
        for part, value in (
            (0, one_re * back_re + one_im * back_im),
            (1, one_re * back_im - one_im * back_re),
        ):
            rim_one_ref[slot, part] = value[0:HALF]
            mid_one_ref[slot, part] = value[HALF:WIN]
        back_re, back_im = sandwich(
            cell_re * back_re + cell_im * back_im,
            cell_re * back_im - cell_im * back_re,
            prop_ref,
            True,
        )
        zero_re, zero_im = wave_ref[slot, 0, 0], wave_ref[slot, 0, 1]
        for part, value in (
            (0, zero_re * back_re + zero_im * back_im),
            (1, zero_re * back_im - zero_im * back_re),
        ):
            rim_zero_ref[slot, part] = value[0:HALF]
            mid_zero_ref[slot, part] = value[HALF:WIN]

    @pl.when(live_slots == 1)
    def _():
        for ref in (rim_zero_ref, rim_one_ref, mid_zero_ref, mid_one_ref):
            ref[1] = jnp.zeros_like(ref[1])


def add_piece(out_ref, piece_ref, column, keep):
    first = lax.shift_right_logical(column, 7)
    offset = jnp.bitwise_and(column, HALF - 1)
    mine = lax.broadcasted_iota(jnp.int32, (CHUNK, HALF), 1) >= offset
    third = jnp.minimum(first + 2, out_ref.shape[-1] // HALF - 1)
    left = piece_ref[:, 0:HALF]
    right = piece_ref[:, HALF:WIN]
    if keep is not None:
        left = jnp.where(keep, left, 0.0)
        right = jnp.where(keep, right, 0.0)
    out_ref[:, block(first)] += jnp.where(mine, left, 0.0)
    out_ref[:, block(first + 1)] += right
    out_ref[:, block(third)] += jnp.where(mine, 0.0, left)


def collect_kernel(
    pos_ref,
    first_ref,
    second_ref,
    first_copy_ref,
    second_copy_ref,
    mid_zero_ref,
    first_zero_ref,
    second_zero_ref,
    first_one_ref,
    second_one_ref,
    mid_one_ref,
    out_ref,
    sum_ref,
    sem,
):
    core = lax.axis_index("cuts")
    tile = lax.axis_index("tile")
    odd = jnp.bitwise_and(tile, 1)
    rows = lax.broadcasted_iota(jnp.int32, (CHUNK, HALF), 0)

    def gather(mid_ref, *nearby):
        copies = []
        columns = [entry(pos_ref, slot, 1) for slot in range(2)]
        places = [
            [(entry(place_ref, slot, 0), entry(place_ref, slot, 1)) for slot in range(2)]
            for _, place_ref, _ in nearby
        ]
        for part in range(2):
            for top in range(0, HALF, CHUNK):
                here = pl.ds(top, CHUNK)
                total = sum_ref.at[part, here]
                total[...] = jnp.zeros(total.shape, jnp.float32)
                for slot in range(2):
                    add_piece(total, mid_ref.at[slot, part, here], columns[slot], None)
                for (piece_ref, _, above), place in zip(nearby, places):
                    sign = 2 * above - 1
                    for slot in range(2):
                        shift_rows = place[slot][0] - (tile + sign - 1) * HALF - top
                        keep = sign * (rows - shift_rows) >= 1 - above
                        piece = piece_ref.at[slot, part, here]
                        add_piece(total, piece, place[slot][1], keep)
                copy = pltpu.make_async_copy(
                    total, out_ref.at[0, part, here], sem.at[len(copies)]
                )
                copy.start()
                copies.append(copy)
        for copy in copies:
            copy.wait()

    @pl.when(core == 0)
    def _():
        gather(
            mid_zero_ref,
            (first_zero_ref, first_copy_ref, odd),
            (second_zero_ref, second_copy_ref, 1 - odd),
        )

    @pl.when(core == 1)
    def _():
        gather(
            mid_one_ref,
            (first_one_ref, first_ref, odd),
            (second_one_ref, second_ref, 1 - odd),
        )


SMEM = pl.BlockSpec(memory_space=pltpu.SMEM)
VMEM = pl.BlockSpec(memory_space=pltpu.VMEM)
ANY = pl.BlockSpec(memory_space=pl.ANY)


LIMIT = 12 << 20


def local(object_slices, probe, positions, counts, intensity):
    tiles = lax.axis_size("tile")

    def first(tile):
        return ((tile + 1) ^ 1) - 1

    def second(tile):
        return tile ^ 1

    def same(tile):
        return tile

    def send(value, source, target, partner):
        pairs = [(tile, partner(tile)) for tile in range(tiles) if 0 <= partner(tile) < tiles]
        pairs = [(source * tiles + one, target * tiles + two) for one, two in pairs]
        return lax.ppermute(value, ("cuts", "tile"), pairs)

    def kernel(body, name, out_shape, in_specs, flops, moved, scratch=(), out_specs=None):
        return pl.pallas_call(
            body,
            out_shape=out_shape,
            in_specs=in_specs,
            out_specs=VMEM if out_specs is None else out_specs,
            scratch_shapes=scratch,
            compiler_params=pltpu.CompilerParams(vmem_limit_bytes=LIMIT),
            cost_estimate=pl.CostEstimate(flops=flops, bytes_accessed=moved, transcendentals=0),
            name=name,
        )

    pieces = jax.ShapeDtypeStruct((2, 2, HALF, WIN), jnp.float32)
    strip = jax.ShapeDtypeStruct(object_slices.shape, jnp.float32)
    window = (pltpu.VMEM((2, WIN, WIN), jnp.float32),)
    tables = jnp.asarray(np.stack(build_tables()))
    other_slice = lax.ppermute(object_slices, "cuts", [(0, 1), (1, 0)])
    pos_first = send(positions, 1, 1, first)
    pos_second = send(positions, 1, 1, second)
    own_slice = kernel(
        stage_kernel, "stage", strip, [ANY], 0, 4 << 20, (pltpu.SemaphoreType.DMA,)
    )(object_slices)

    def cut(name, source):
        return kernel(
            cut_kernel, name, (pieces,) * 2, [VMEM] * 2 + [VMEM], 0, 2 << 20, (), (VMEM,) * 2
        )(pos_first, pos_second, source)

    to_first_zero, to_second_zero = cut("cut_zero", other_slice)
    second_zero = send(to_second_zero, 1, 0, second)
    first_zero = send(to_first_zero, 1, 0, first)
    to_first_one, to_second_one = cut("cut_one", own_slice)
    second_one = send(to_second_one, 1, 0, second)
    first_one = send(to_first_one, 1, 0, first)
    second_copy = send(pos_second, 1, 0, same)
    first_copy = send(pos_first, 1, 0, same)
    wave = kernel(
        enter_kernel,
        "enter",
        jax.ShapeDtypeStruct((2, 2, 2, WIN, WIN), jnp.float32),
        [VMEM, SMEM] + [VMEM] * 5 + [ANY] * 2,
        18 * 2 * WIN**3,
        3 << 20,
        window,
    )(positions, counts, probe, tables, own_slice, first_zero, second_zero, first_copy, second_copy)
    rim_zero, rim_one, mid_zero, mid_one = kernel(
        slot_kernel,
        "slot",
        (pieces,) * 4,
        [VMEM, SMEM] + [VMEM] * 6,
        54 * 2 * WIN**3,
        6 << 20,
        window,
        (VMEM,) * 4,
    )(positions, counts, tables, wave, other_slice, first_one, second_one, intensity)
    back_first_zero = send(rim_zero, 0, 1, first)
    back_second_zero = send(rim_zero, 0, 1, second)
    back_first_one = send(rim_one, 0, 1, first)
    back_second_one = send(rim_one, 0, 1, second)
    mid_one = send(mid_one, 0, 1, same)
    return kernel(
        collect_kernel,
        "collect",
        strip,
        [VMEM] * 11,
        0,
        4 << 20,
        (pltpu.VMEM(strip.shape[1:], jnp.float32), pltpu.SemaphoreType.DMA((2 * HALF // CHUNK,))),
        ANY,
    )(
        positions,
        pos_first,
        pos_second,
        first_copy,
        second_copy,
        mid_zero,
        send(back_first_zero, 1, 0, same),
        send(back_second_zero, 1, 0, same),
        back_first_one,
        back_second_one,
        mid_one,
    )


def solution(mesh):
    in_specs = (
        P("cuts", None, "tile", None),
        P(),
        P("tile", None),
        P("tile"),
        P("tile", None, None),
    )
    out_specs = P("cuts", None, "tile", None)
    return jax.shard_map(local, mesh=mesh, in_specs=in_specs, out_specs=out_specs, check_vma=False)
```

```python
import numpy as np
import ml_dtypes

import jax
import jax.numpy as jnp
from jax import lax
from jax.experimental import pallas as pl
from jax.experimental.pallas import tpu as pltpu
from jax.sharding import PartitionSpec as P

WIN = 256
HALF = 128
CHUNK = 128


def split_tables(real_part, imag_part):
    parts = []
    for values in (real_part, imag_part, -imag_part):
        high = values.astype(ml_dtypes.bfloat16)
        low = (values - high.astype(np.float64)).astype(ml_dtypes.bfloat16)
        parts += [high, low]
    return np.stack(parts)


def build_tables():
    index = np.arange(WIN)
    turned = 2.0 * np.pi * ((index[:, None] * index[None, :]) % WIN) / WIN
    dft = (np.cos(turned) - 1j * np.sin(turned)) / np.sqrt(WIN)
    centred = (index + WIN // 2) % WIN - WIN // 2
    phase = np.pi * (centred * centred % (4 * WIN)) / (2 * WIN)
    prop = np.conj(dft) @ ((np.cos(phase) - 1j * np.sin(phase))[:, None] * dft)
    prop = 0.5 * (prop + prop.T)
    return split_tables(dft.real, dft.imag), split_tables(prop.real, prop.imag)


def split(value):
    high = value.astype(jnp.bfloat16)
    low = (value - high.astype(jnp.float32)).astype(jnp.bfloat16)
    return high, low


def dot(left, right):
    return jnp.dot(left, right, preferred_element_type=jnp.float32)


def complex_product(real, imag, table, conjugate, from_left):
    real_high, real_low = split(real)
    imag_high, imag_low = split(imag)
    fields = [real_high, real_low, real_high, imag_high, imag_low, imag_high]

    def terms(which):
        return [table[2 * which], table[2 * which], table[2 * which + 1]]

    plus, minus = (2, 1) if conjugate else (1, 2)
    results = []
    for parts in (terms(0) + terms(minus), terms(plus) + terms(0)):
        if from_left:
            left, right = jnp.concatenate(parts, axis=1), jnp.concatenate(fields, axis=0)
        else:
            left, right = jnp.concatenate(fields, axis=1), jnp.concatenate(parts, axis=0)
        results.append(dot(left, right))
    return results


def sandwich(real, imag, table, conjugate):
    real, imag = complex_product(real, imag, table, conjugate, False)
    return complex_product(real, imag, table, conjugate, True)


def block(number):
    return pl.ds(pl.multiple_of(number * HALF, HALF), HALF)


def entry(ref, slot, which):
    rows = lax.broadcasted_iota(jnp.int32, (2, 2), 0)
    columns = lax.broadcasted_iota(jnp.int32, (2, 2), 1)
    values = ref[...].astype(jnp.float32)
    chosen = jnp.where((rows == slot) & (columns == which), values, 0.0)
    return jnp.sum(chosen).astype(jnp.int32)


def cut_piece(strip_ref, column, out_ref):
    first = lax.shift_right_logical(column, 7)
    offset = jnp.bitwise_and(column, HALF - 1)
    lanes = lax.broadcasted_iota(jnp.int32, (HALF, HALF), 1)
    mine = lanes >= offset
    third = jnp.minimum(first + 2, strip_ref.shape[-1] // HALF - 1)
    for part in range(2):
        out_ref[part, :, 0:HALF] = jnp.where(
            mine, strip_ref[0, part, :, block(first)], strip_ref[0, part, :, block(third)]
        )
        out_ref[part, :, HALF:WIN] = strip_ref[0, part, :, block(first + 1)]


def stage_kernel(strip_ref, out_ref, sem):
    copy = pltpu.make_async_copy(strip_ref, out_ref, sem)
    copy.start()
    copy.wait()


def cut_kernel(first_ref, second_ref, strip_ref, to_first_ref, to_second_ref):
    @pl.when(lax.axis_index("cuts") == 1)
    def _():
        for slot in range(2):
            cut_piece(strip_ref, entry(first_ref, slot, 1), to_first_ref.at[slot])
        for slot in range(2):
            cut_piece(strip_ref, entry(second_ref, slot, 1), to_second_ref.at[slot])


def slots_of_core(counts_ref):
    return jnp.where(lax.axis_index("cuts") == 0, counts_ref[0], 0)


def fill_window(pos_ref, slot, strip_ref, first_ref, second_ref, window_ref):
    tile = lax.axis_index("tile")
    odd = jnp.bitwise_and(tile, 1)
    shift_rows = entry(pos_ref, slot, 0) - (tile - 1) * HALF
    column = entry(pos_ref, slot, 1)
    rows = lax.broadcasted_iota(jnp.int32, (HALF, WIN), 0)
    from_first = (1 - 2 * odd) * (rows - shift_rows) >= odd
    for part in range(2):
        window_ref[part, 0:HALF] = jnp.where(
            from_first, first_ref[slot, part], second_ref[slot, part]
        )
    cut_piece(strip_ref, column, window_ref.at[:, HALF:WIN])
    return shift_rows, jnp.bitwise_and(column, HALF - 1)


def enter_kernel(
    pos_ref,
    counts_ref,
    probe_ref,
    table_ref,
    own_ref,
    first_ref,
    second_ref,
    first_copy_ref,
    second_copy_ref,
    wave_ref,
    window_ref,
):
    @pl.loop(0, slots_of_core(counts_ref))
    def _(slot):
        shift_rows, shift_cols = fill_window(pos_ref, slot, own_ref, first_ref, second_ref, window_ref)

        def rolled(part):
            return pltpu.roll(pltpu.roll(probe_ref[part], shift_rows, 0), shift_cols, 1)

        zero_re, zero_im = rolled(0), rolled(1)
        wave_ref[slot, 0, 0] = zero_re
        wave_ref[slot, 0, 1] = zero_im
        cell_re, cell_im = window_ref[0], window_ref[1]
        one_re, one_im = sandwich(
            zero_re * cell_re - zero_im * cell_im,
            zero_re * cell_im + zero_im * cell_re,
            table_ref.at[1],
            False,
        )
        wave_ref[slot, 1, 0] = one_re
        wave_ref[slot, 1, 1] = one_im


def slot_kernel(
    pos_ref,
    counts_ref,
    table_ref,
    wave_ref,
    other_ref,
    first_ref,
    second_ref,
    intensity_ref,
    rim_zero_ref,
    rim_one_ref,
    mid_zero_ref,
    mid_one_ref,
    window_ref,
):
    live_slots = slots_of_core(counts_ref)
    dft_ref, prop_ref = table_ref.at[0], table_ref.at[1]

    @pl.loop(0, live_slots)
    def _(slot):
        fill_window(pos_ref, slot, other_ref, first_ref, second_ref, window_ref)
        cell_re, cell_im = window_ref[0], window_ref[1]
        one_re, one_im = wave_ref[slot, 1, 0], wave_ref[slot, 1, 1]
        far_re, far_im = sandwich(
            one_re * cell_re - one_im * cell_im,
            one_re * cell_im + one_im * cell_re,
            dft_ref,
            False,
        )
        residual = far_re * far_re + far_im * far_im - intensity_ref[slot]
        back_re, back_im = sandwich(far_re * residual, far_im * residual, dft_ref, True)
        for part, value in (
            (0, one_re * back_re + one_im * back_im),
            (1, one_re * back_im - one_im * back_re),
        ):
            rim_one_ref[slot, part] = value[0:HALF]
            mid_one_ref[slot, part] = value[HALF:WIN]
        back_re, back_im = sandwich(
            cell_re * back_re + cell_im * back_im,
            cell_re * back_im - cell_im * back_re,
            prop_ref,
            True,
        )
        zero_re, zero_im = wave_ref[slot, 0, 0], wave_ref[slot, 0, 1]
        for part, value in (
            (0, zero_re * back_re + zero_im * back_im),
            (1, zero_re * back_im - zero_im * back_re),
        ):
            rim_zero_ref[slot, part] = value[0:HALF]
            mid_zero_ref[slot, part] = value[HALF:WIN]

    @pl.when(live_slots == 1)
    def _():
        for ref in (rim_zero_ref, rim_one_ref, mid_zero_ref, mid_one_ref):
            ref[1] = jnp.zeros_like(ref[1])


def add_piece(out_ref, piece_ref, column, keep):
    first = lax.shift_right_logical(column, 7)
    offset = jnp.bitwise_and(column, HALF - 1)
    mine = lax.broadcasted_iota(jnp.int32, (CHUNK, HALF), 1) >= offset
    third = jnp.minimum(first + 2, out_ref.shape[-1] // HALF - 1)
    left = piece_ref[:, 0:HALF]
    right = piece_ref[:, HALF:WIN]
    if keep is not None:
        left = jnp.where(keep, left, 0.0)
        right = jnp.where(keep, right, 0.0)
    out_ref[:, block(first)] += jnp.where(mine, left, 0.0)
    out_ref[:, block(first + 1)] += right
    out_ref[:, block(third)] += jnp.where(mine, 0.0, left)


def collect_kernel(
    pos_ref,
    first_ref,
    second_ref,
    first_copy_ref,
    second_copy_ref,
    mid_zero_ref,
    first_zero_ref,
    second_zero_ref,
    first_one_ref,
    second_one_ref,
    mid_one_ref,
    out_ref,
    sum_ref,
    sem,
):
    core = lax.axis_index("cuts")
    tile = lax.axis_index("tile")
    odd = jnp.bitwise_and(tile, 1)
    rows = lax.broadcasted_iota(jnp.int32, (CHUNK, HALF), 0)

    def gather(mid_ref, *nearby):
        copies = []
        columns = [entry(pos_ref, slot, 1) for slot in range(2)]
        places = [
            [(entry(place_ref, slot, 0), entry(place_ref, slot, 1)) for slot in range(2)]
            for _, place_ref, _ in nearby
        ]
        for part in range(2):
            for top in range(0, HALF, CHUNK):
                here = pl.ds(top, CHUNK)
                total = sum_ref.at[part, here]
                total[...] = jnp.zeros(total.shape, jnp.float32)
                for slot in range(2):
                    add_piece(total, mid_ref.at[slot, part, here], columns[slot], None)
                for (piece_ref, _, above), place in zip(nearby, places):
                    sign = 2 * above - 1
                    for slot in range(2):
                        shift_rows = place[slot][0] - (tile + sign - 1) * HALF - top
                        keep = sign * (rows - shift_rows) >= 1 - above
                        piece = piece_ref.at[slot, part, here]
                        add_piece(total, piece, place[slot][1], keep)
                copy = pltpu.make_async_copy(
                    total, out_ref.at[0, part, here], sem.at[len(copies)]
                )
                copy.start()
                copies.append(copy)
        for copy in copies:
            copy.wait()

    @pl.when(core == 0)
    def _():
        gather(
            mid_zero_ref,
            (first_zero_ref, first_copy_ref, odd),
            (second_zero_ref, second_copy_ref, 1 - odd),
        )

    @pl.when(core == 1)
    def _():
        gather(
            mid_one_ref,
            (first_one_ref, first_ref, odd),
            (second_one_ref, second_ref, 1 - odd),
        )


SMEM = pl.BlockSpec(memory_space=pltpu.SMEM)
VMEM = pl.BlockSpec(memory_space=pltpu.VMEM)
ANY = pl.BlockSpec(memory_space=pl.ANY)


LIMIT = 12 << 20


def local(object_slices, probe, positions, counts, intensity):
    tiles = lax.axis_size("tile")

    def first(tile):
        return ((tile + 1) ^ 1) - 1

    def second(tile):
        return tile ^ 1

    def same(tile):
        return tile

    def send(value, source, target, partner):
        pairs = [(tile, partner(tile)) for tile in range(tiles) if 0 <= partner(tile) < tiles]
        pairs = [(source * tiles + one, target * tiles + two) for one, two in pairs]
        return lax.ppermute(value, ("cuts", "tile"), pairs)

    def kernel(body, name, out_shape, in_specs, flops, moved, scratch=(), out_specs=None):
        return pl.pallas_call(
            body,
            out_shape=out_shape,
            in_specs=in_specs,
            out_specs=VMEM if out_specs is None else out_specs,
            scratch_shapes=scratch,
            compiler_params=pltpu.CompilerParams(vmem_limit_bytes=LIMIT),
            cost_estimate=pl.CostEstimate(flops=flops, bytes_accessed=moved, transcendentals=0),
            name=name,
        )

    pieces = jax.ShapeDtypeStruct((2, 2, HALF, WIN), jnp.float32)
    strip = jax.ShapeDtypeStruct(object_slices.shape, jnp.float32)
    window = (pltpu.VMEM((2, WIN, WIN), jnp.float32),)
    tables = jnp.asarray(np.stack(build_tables()))
    other_slice = lax.ppermute(object_slices, "cuts", [(0, 1), (1, 0)])
    pos_first = send(positions, 1, 1, first)
    pos_second = send(positions, 1, 1, second)
    own_slice = kernel(
        stage_kernel, "stage", strip, [ANY], 0, 4 << 20, (pltpu.SemaphoreType.DMA,)
    )(object_slices)

    def cut(name, source):
        return kernel(
            cut_kernel, name, (pieces,) * 2, [VMEM] * 2 + [VMEM], 0, 2 << 20, (), (VMEM,) * 2
        )(pos_first, pos_second, source)

    to_first_zero, to_second_zero = cut("cut_zero", other_slice)
    second_zero = send(to_second_zero, 1, 0, second)
    first_zero = send(to_first_zero, 1, 0, first)
    to_first_one, to_second_one = cut("cut_one", own_slice)
    second_one = send(to_second_one, 1, 0, second)
    first_one = send(to_first_one, 1, 0, first)
    second_copy = send(pos_second, 1, 0, same)
    first_copy = send(pos_first, 1, 0, same)
    wave = kernel(
        enter_kernel,
        "enter",
        jax.ShapeDtypeStruct((2, 2, 2, WIN, WIN), jnp.float32),
        [VMEM, SMEM] + [VMEM] * 5 + [ANY] * 2,
        18 * 2 * WIN**3,
        3 << 20,
        window,
    )(positions, counts, probe, tables, own_slice, first_zero, second_zero, first_copy, second_copy)
    rim_zero, rim_one, mid_zero, mid_one = kernel(
        slot_kernel,
        "slot",
        (pieces,) * 4,
        [VMEM, SMEM] + [VMEM] * 6,
        54 * 2 * WIN**3,
        6 << 20,
        window,
        (VMEM,) * 4,
    )(positions, counts, tables, wave, other_slice, first_one, second_one, intensity)
    back_first_zero = send(rim_zero, 0, 1, first)
    back_second_zero = send(rim_zero, 0, 1, second)
    back_first_one = send(rim_one, 0, 1, first)
    back_second_one = send(rim_one, 0, 1, second)
    mid_one = send(mid_one, 0, 1, same)
    return kernel(
        collect_kernel,
        "collect",
        strip,
        [VMEM] * 11,
        0,
        4 << 20,
        (pltpu.VMEM(strip.shape[1:], jnp.float32), pltpu.SemaphoreType.DMA((2 * HALF // CHUNK,))),
        ANY,
    )(
        positions,
        pos_first,
        pos_second,
        first_copy,
        second_copy,
        mid_zero,
        send(back_first_zero, 1, 0, same),
        send(back_second_zero, 1, 0, same),
        back_first_one,
        back_second_one,
        mid_one,
    )


def solution(mesh):
    in_specs = (
        P("cuts", None, "tile", None),
        P(),
        P("tile", None),
        P("tile"),
        P("tile", None, None),
    )
    out_specs = P("cuts", None, "tile", None)
    return jax.shard_map(local, mesh=mesh, in_specs=in_specs, out_specs=out_specs, check_vma=False)
```
